32 devices in a mesh: groups: 2 (over x), ctx: 16 (over z, y, core).
Axes of the slice: x: 2, y: 2, z: 4, core: 2. Of those that a mesh axis runs over, the one named last changes fastest.
Arguments:
- gate_short: bfloat16 [4096, 4096], P(('groups', 'ctx')), parts along dimension 0, may hold values from -6 to 6
- key_short: bfloat16 [4096, 4096], P(('groups', 'ctx')), parts along dimension 0, may hold values from -6 to 6
- value_short: bfloat16 [4096, 4096], P(('groups', 'ctx')), parts along dimension 0, may hold values from -6 to 6
- gate_long: bfloat16 [4096, 4096], P(('groups', 'ctx')), parts along dimension 0, may hold values from -6 to 6
- doc_ids: int32 [4096], P(('groups', 'ctx')), parts along dimension 0, may hold values from 0 to 7, never falling along the last dimension, each value on 1 to 512 neighbouring positions
- se_filter: float32 [7, 256], replicated, may hold values from -2 to 2
- long_filter: bfloat16 [256, 512], replicated, may hold values from -1.25 to 1.25
Outputs:
- scored: bfloat16 [4096, 4096], P(('groups', 'ctx')), parts along dimension 0
The draws below stay inside these ranges and needn't reach their ends.
There are 2 independent parts, one for each index of `groups`. The reference program is written for one: setup_inputs(seed, part) draws one part's arguments, and reference() takes and returns one part's arrays. A program takes and returns all parts, laid end to end along the dimension named above; an argument that names none is the same for every part. Nothing has to cross between parts.
Inputs may be any that keep to these rules, and one draw needn't show every extreme that they name: doc_ids never falls along the rows of a group; each document holds 1 to 512 consecutive rows, and one holds exactly 512.
All inputs are finite; a program needn't handle non-finite values.
Results may differ from the reference program's by a relative error of at most 0.0057.
Values may be sent and summed in bfloat16 or wider, within the bound.
A program may use at most 192 MiB of HBM per device.

```python
import math
import jax
import jax.numpy as jnp
import numpy as np
from jax import lax

C = 4096
FGROUP = 16
SHORT_TAPS = 7
STRETCH = 128
MAXDOC = 512
FILTERS = 256
TOKENS = 2048
DOCS = 8


def draw_long_filter(key, part):
    key_noise = jax.random.fold_in(key, 11)
    key_decay = jax.random.fold_in(key, 12)
    lag_axis = jnp.arange(MAXDOC, dtype=jnp.float32)[None, :]
    noise_draw = jax.random.truncated_normal(key_noise, -3.0, 3.0, (FILTERS, MAXDOC), jnp.float32)
    log_lowest = jnp.log(12.0)
    log_highest = jnp.log(8.0 * MAXDOC)
    decay_length = jnp.exp(jax.random.uniform(key_decay, (FILTERS, 1), jnp.float32, log_lowest, log_highest))
    norm_scale = jnp.sqrt(2.0 / jnp.minimum(decay_length, 1.0 * MAXDOC))
    return (noise_draw * jnp.exp(-lag_axis / decay_length) * norm_scale).astype(jnp.bfloat16)


def steps_of(stream_key, extent, pieces, least, top_value):
    gain, own = 1.0, jax.random.fold_in(stream_key, 6)
    for axis_at, shards_of in pieces:
        heights = jnp.exp(jax.random.uniform(jax.random.fold_in(own, axis_at), (shards_of,), jnp.float32, least / len(pieces), top_value / len(pieces)))
        gain = gain * jnp.repeat(heights, extent[axis_at] // shards_of).reshape([-1 if axis == axis_at else 1 for axis in range(len(extent))])
    return gain


def split_up(count, total, most, lean):
    loads = [(1 << 20) // math.isqrt(grade ** lean) + 1 for grade in range(2, count + 1)]
    surplus, counts = total - most - (count - 1), [1] * (count - 1)
    while surplus > 0:
        free = [i for i in range(count - 1) if counts[i] < most]
        mass, remaining = sum([loads[i] for i in free]), surplus
        for i in free:
            extra = min(most - counts[i], max(1, remaining * loads[i] // mass), surplus)
            counts[i] = counts[i] + extra
            surplus = surplus - extra
    return np.array([most] + counts)


def ragged_sizes(own_key, number_of, total, limit, skew):
    if number_of == 2:
        one = jax.random.randint(own_key, (), max(1, total - limit), min(limit, total - 1) + 1)
        return jnp.stack([one, total - one])
    sizes = jnp.asarray(split_up(number_of, total, limit, skew), jnp.int32)
    couples = (number_of - 1) // 2
    source_of, sink = sizes[1:1 + 2 * couples:2], sizes[2:2 + 2 * couples:2]
    slack = jnp.minimum(source_of - 1, limit - sink)
    moved = jax.random.randint(jax.random.fold_in(own_key, 1), (couples,), 0, 1 << 20) % (slack + 1)
    sizes = sizes.at[1:1 + 2 * couples:2].set(source_of - moved).at[2:2 + 2 * couples:2].set(sink + moved)
    return sizes[jax.random.permutation(jax.random.fold_in(own_key, 2), number_of)]


def gaussian(rng, extent, deviation, bound, cuts=(), kind=jnp.bfloat16):
    entries = deviation * jax.random.normal(rng, extent, jnp.float32)
    if cuts:
        entries = entries * steps_of(rng, extent, cuts, -0.22, 0.18)
    return jnp.clip(entries, -bound, bound).astype(kind)


def setup_inputs(seed: int = 0, part: int = 0) -> dict:
    seeds = jax.random.split(jax.random.key(seed), 8)
    part_splits = jax.random.split(jax.random.fold_in(seeds[7], part), 8)
    gate_short = gaussian(part_splits[0], (TOKENS, C), 1.0, 6.0, ((0, 16),))
    key_short = gaussian(part_splits[1], (TOKENS, C), 1.0, 6.0, ((0, 16),))
    value_short = gaussian(part_splits[2], (TOKENS, C), 1.0, 6.0, ((0, 16),))
    gate_long = gaussian(part_splits[3], (TOKENS, C), 1.0, 6.0, ((0, 16),))
    doc_ids = jnp.searchsorted(jnp.cumsum(ragged_sizes(part_splits[4], DOCS, TOKENS, MAXDOC, 2)), jnp.arange(TOKENS), side="right").astype(jnp.int32)
    se_filter = gaussian(seeds[5], (SHORT_TAPS, FILTERS), SHORT_TAPS ** -0.5, 2.0, (), jnp.float32)
    long_filter = draw_long_filter(jax.random.fold_in(seeds[7], 71), part)
    return dict(gate_short=gate_short, key_short=key_short, value_short=value_short, gate_long=gate_long, doc_ids=doc_ids, se_filter=se_filter, long_filter=long_filter)


def short_mixing(key_value, doc_ids, se_filter):
    row_count = key_value.shape[0]
    widened = jnp.repeat(se_filter, FGROUP, axis=1)
    values = key_value.astype(jnp.float32)
    summed = jnp.zeros(values.shape, jnp.float32)
    for tap_index in range(SHORT_TAPS):
        shifted = jnp.concatenate([jnp.zeros((tap_index, values.shape[1]), jnp.float32), values], 0)[:row_count]
        shifted_doc = jnp.concatenate([jnp.full((tap_index,), -1, jnp.int32), doc_ids], 0)[:row_count]
        agreeing = (shifted_doc == doc_ids).astype(jnp.float32)
        summed = summed + widened[tap_index][None, :] * agreeing[:, None] * shifted
    return summed


def long_mixing(mixed, doc_ids, long_filter):
    row_count, chan_count = mixed.shape
    filter_count = long_filter.shape[0]
    window = (MAXDOC // STRETCH + 1) * STRETCH
    front_rows = window - STRETCH
    padded = jnp.concatenate([jnp.zeros((front_rows, chan_count), mixed.dtype), mixed], 0)
    padded_doc = jnp.concatenate([jnp.full((front_rows,), -1, jnp.int32), doc_ids], 0)
    target_pos = lax.broadcasted_iota(jnp.int32, (STRETCH, window), 0)
    source_pos = lax.broadcasted_iota(jnp.int32, (STRETCH, window), 1)
    lag_table = target_pos + front_rows - source_pos
    inside = (lag_table >= 0) & (lag_table < MAXDOC)
    filter_taps = jnp.take(long_filter.astype(jnp.float32), jnp.clip(lag_table, 0, MAXDOC - 1), axis=1)
    filter_taps = jnp.where(inside[None], filter_taps, jnp.zeros_like(filter_taps))

    def one_tile(tile_index):
        begin_row = (tile_index * STRETCH).astype(jnp.int32)
        rows_win = lax.dynamic_slice_in_dim(padded, begin_row, window, 0).astype(jnp.float32)
        docs_win = lax.dynamic_slice_in_dim(padded_doc, begin_row, window, 0)
        docs_tgt = lax.dynamic_slice_in_dim(doc_ids, begin_row, STRETCH, 0)
        agreeing = (docs_tgt[:, None] == docs_win[None, :]).astype(jnp.float32)
        weights = filter_taps * agreeing[None]
        result = jnp.einsum("gtp,pgk->tgk", weights, rows_win.reshape(window, filter_count, -1))
        return result.reshape(STRETCH, chan_count)

    tile_results = lax.map(one_tile, jnp.arange(row_count // STRETCH, dtype=jnp.int32))
    return tile_results.reshape(row_count, chan_count)


def reference(gate_short, key_short, value_short, gate_long, doc_ids, se_filter, long_filter):
    key_value = (key_short.astype(jnp.float32) * value_short.astype(jnp.float32)).astype(jnp.bfloat16)
    key_value = lax.optimization_barrier(key_value)
    short_mix = short_mixing(key_value, doc_ids, se_filter)
    mixed = (gate_short.astype(jnp.float32) * short_mix).astype(jnp.bfloat16)
    mixed = lax.optimization_barrier(mixed)
    long_mix = long_mixing(mixed, doc_ids, long_filter)
    return (gate_long.astype(jnp.float32) * long_mix).astype(jnp.bfloat16)
```

```python
import functools

import jax
import jax.numpy as jnp
from jax import lax
from jax.experimental import pallas as pl
from jax.experimental.pallas import tpu as pltpu
from jax.sharding import PartitionSpec as P

MAXDOC = 512
REACH = 4
RIM = 8
LANES = 128
PACK = 16
MSGS = 16
EARLY = 2
LAG1 = 2
LAG2 = 5
BASE = 32
MESH = pl.DeviceIdType.MESH


def kernel(
    count, gs_hbm, k_hbm, v_hbm, gl_hbm, doc_hbm, se_hbm, h_hbm, out_ref,
    gs_ref, k_ref, v_ref, gl_ref, doc_ref, se_ref, h_ref, tail_k, tail_v,
    own, got, doc_out, got_doc, rim_out, rim_in, se_two, doc_ext, ext, agree,
    rev, taps, acc, near_mask, far_mask, out_mask,
    in_sem, one_sem, send_sem, recv_sem, head_send, head_recv, doc_send, doc_recv, rim_send, rim_recv,
):
    rows, chans = gs_ref.shape
    tap_count, filters = se_ref.shape
    fgroup = chans // filters
    per_tile = LANES // fgroup
    tiles = chans // LANES
    each = tiles // MSGS
    width = each * LANES
    half = rows // 2
    body_rows = rows - RIM
    f32, bf16, i32 = jnp.float32, jnp.bfloat16, jnp.int32

    me = lax.axis_index("ctx")
    at = lax.rem(me, REACH)
    core = lax.rem(me, 2)
    upper = at // 2
    core_mate = me + 1 - 2 * core
    row_mate = me + 2 - 4 * upper
    has_prev = me >= REACH
    has_next = me + REACH < count

    def local(src, dst, sem):
        return pltpu.make_async_copy(src, dst, sem)

    def piece(i, j):
        src, dst = ((k_hbm, k_ref), (v_hbm, v_ref), (gs_hbm, gs_ref))[i]
        cols = pl.ds(pl.multiple_of(j * width, width), width)
        return local(src.at[:, cols], dst.at[:, cols], in_sem.at[i, j])

    doc_in = local(doc_hbm, doc_ref, one_sem.at[0])
    tails = [
        local(k_hbm.at[pl.ds(rows - RIM, RIM), :], tail_k, one_sem.at[1]),
        local(v_hbm.at[pl.ds(rows - RIM, RIM), :], tail_v, one_sem.at[2]),
    ]
    se_in = local(se_hbm, se_ref, one_sem.at[3])
    h_in = local(h_hbm, h_ref, one_sem.at[4])
    gl_in = local(gl_hbm, gl_ref, one_sem.at[5])

    doc_in.start()
    tails[0].start()
    tails[1].start()
    se_in.start()
    for i in range(3):
        piece(i, 0).start()

    barrier = pltpu.get_barrier_semaphore()

    def greet(target):
        pl.semaphore_signal(barrier, inc=1, device_id={"ctx": target}, device_id_type=MESH)

    peers = jnp.int32(0)
    for d in range(1, REACH + 1):
        pl.when(me >= d)(lambda d=d: greet(me - d))
        pl.when(me + d < count)(lambda d=d: greet(me + d))
        peers = peers + (me >= d).astype(i32) + (me + d < count).astype(i32)

    def fetch(j, _):
        for i in range(3):
            piece(i, j).start()
        return 0

    lax.fori_loop(1, MSGS, fetch, 0)
    h_in.start()
    gl_in.start()

    lane = lax.broadcasted_iota(i32, (rows, LANES), 1)
    row = lax.broadcasted_iota(i32, (rows, LANES), 0)

    doc_in.wait()
    doc_row = jnp.broadcast_to(doc_ref[...].astype(f32), (rows, LANES))
    doc_col = doc_row.T
    doc_out[...] = doc_row[0:8]
    doc_ext[RIM:, :] = doc_col
    tails[0].wait()
    tails[1].wait()
    rim_out[...] = (tail_k[...].astype(f32) * tail_v[...].astype(f32)).astype(bf16)

    pl.semaphore_wait(barrier, peers)

    def remote(src, dst, ssem, rsem, target):
        return pltpu.make_async_remote_copy(
            src_ref=src, dst_ref=dst, send_sem=ssem, recv_sem=rsem,
            device_id={"ctx": target}, device_id_type=MESH,
        )

    def rim_copy(target):
        return remote(rim_out, rim_in, rim_send, rim_recv, target)

    def doc_copy(d, target):
        slot = REACH - d
        return remote(doc_out, got_doc.at[slot], doc_send.at[slot], doc_recv.at[slot], target)

    pl.when(me + 1 < count)(lambda: rim_copy(me + 1).start())
    for d in range(1, REACH + 1):
        pl.when(me + d < count)(lambda d=d: doc_copy(d, me + d).start())

    def msg_copy(slot, m, source, target):
        block = own if source is None else got.at[source]
        part = (pl.ds(m * each, each), pl.ds(RIM, body_rows))
        return remote(block.at[part], got.at[(slot, *part)], send_sem.at[slot, m], recv_sem.at[slot, m], target)

    def head_copy(slot, source, target):
        block = own if source is None else got.at[source]
        part = (pl.ds(0, tiles), pl.ds(0, RIM))
        return remote(block.at[part], got.at[(slot, *part)], head_send.at[slot], head_recv.at[slot], target)

    def send_own(copy):
        pl.when(has_next)(lambda: copy(0, None, me + REACH).start())
        pl.when(upper == 0)(lambda: copy(2, None, row_mate).start())
        pl.when(core == 0)(lambda: copy(1, None, core_mate).start())

    def msg(m):
        return lambda slot, source, target: msg_copy(slot, m, source, target)

    for tap in range(1, tap_count):
        agree[tap, RIM:, :] = (doc_ext[2 * RIM - tap : RIM + rows - tap, :] == doc_col[RIM:]).astype(f32)

    se_in.wait()
    for part in range(filters // LANES):
        se_two[part, 0:tap_count, :] = se_ref[:, part * LANES : (part + 1) * LANES]
        se_two[part, tap_count:, :] = jnp.zeros((8 - tap_count, LANES), f32)

    tiles_per_part = LANES // per_tile
    spread = lax.broadcasted_iota(i32, (8, LANES), 1) // fgroup

    def weights_of(ct):
        index = spread + lax.rem(ct, tiles_per_part) * per_tile
        return jnp.take_along_axis(se_two[ct // tiles_per_part], index, axis=1)

    def lanes_of(ct):
        return pl.ds(pl.multiple_of(ct * LANES, LANES), LANES)

    def product(ct, part):
        lanes = lanes_of(ct)
        return (k_ref[part, lanes].astype(f32) * v_ref[part, lanes].astype(f32)).astype(bf16).astype(f32)

    def short_body(j, _):
        for i in range(3):
            piece(i, j).wait()
        for u in range(each):
            ct = j * each + u
            weights = weights_of(ct)
            kv = product(ct, slice(None))
            ext[u, RIM:, :] = kv
            total = kv[RIM:] * weights[0:1, :]
            for tap in range(1, tap_count):
                shifted = ext[u, 2 * RIM - tap : RIM + rows - tap, :]
                total = total + (shifted * agree[tap, RIM:, :]) * weights[tap : tap + 1, :]
            mixed = gs_ref[RIM:, lanes_of(ct)].astype(f32) * total
            own[ct, RIM:, :] = mixed.astype(bf16)
        pl.when(j < EARLY)(lambda: send_own(msg(j)))
        return 0

    lax.fori_loop(0, MSGS, short_body, 0)

    h_in.wait()
    lag = lax.broadcasted_iota(i32, (LANES, LANES), 0)
    pos = lax.broadcasted_iota(i32, (LANES, LANES), 1)
    flip = jnp.where(lag == lax.rem(LANES - pos, LANES), 1.0, 0.0).astype(bf16)
    for d in range(REACH):
        cols = slice(d * LANES, (d + 1) * LANES)
        rev[:, cols] = jnp.dot(h_ref[:, cols], flip, preferred_element_type=f32)

    low = lane[:half] < half
    causal = lane[:half] <= row[:half]
    same_low = doc_col[:half] == doc_row[:half]
    same_high = doc_col[half:] == pltpu.roll(doc_row[:half], half, 1)
    late = same_high.astype(f32)
    early = causal.astype(f32) * same_low.astype(f32)
    near_mask[0] = jnp.where(low, early, late).astype(bf16)
    near_mask[1] = jnp.where(low, causal.astype(f32) * late, 0.0).astype(bf16)
    leader = jnp.broadcast_to(doc_row[0:1, 0:1], (rows, LANES))
    out_mask[...] = (doc_col == leader).astype(f32)

    for w in range(REACH):
        pl.when(me >= REACH - w)(lambda w=w: doc_copy(REACH - w, core_mate).wait_recv())

        @pl.when(me < REACH - w)
        def _():
            got_doc[w] = jnp.full((8, LANES), -1.0, f32)

        source_col = jnp.broadcast_to(got_doc[w, 0:1, :], (rows, LANES)).T
        far_mask[w] = (source_col == leader).astype(bf16)
        if w == REACH - 1:
            doc_ext[0:RIM, :] = source_col[rows - RIM :]

    @pl.when(me == 0)
    def _():
        rim_in[...] = jnp.zeros((RIM, chans), bf16)

    @pl.when(me > 0)
    def _():
        rim_copy(core_mate).wait_recv()

    for tap in range(1, tap_count):
        agree[tap, 0:RIM, :] = (doc_ext[RIM - tap : 2 * RIM - tap, :] == doc_col[0:RIM]).astype(f32)

    def short_head(j, _):
        for u in range(4):
            ct = j * 4 + u
            weights = weights_of(ct)
            kv = product(ct, slice(0, RIM))
            ext[u, 0:RIM, :] = rim_in[:, lanes_of(ct)].astype(f32)
            ext[u, RIM : 2 * RIM, :] = kv
            total = kv * weights[0:1, :]
            for tap in range(1, tap_count):
                shifted = ext[u, RIM - tap : 2 * RIM - tap, :]
                total = total + (shifted * agree[tap, 0:RIM, :]) * weights[tap : tap + 1, :]
            mixed = gs_ref[0:RIM, lanes_of(ct)].astype(f32) * total
            own[ct, 0:RIM, :] = mixed.astype(bf16)
        return 0

    lax.fori_loop(0, tiles // 4, short_head, 0)
    send_own(head_copy)

    def send_rest(j, _):
        send_own(msg(j))
        return 0

    lax.fori_loop(EARLY, MSGS, send_rest, 0)

    @pl.when(jnp.logical_not(has_prev))
    def _():
        got[0] = jnp.zeros(got.shape[1:], bf16)

    gl_in.wait()

    tile_group = lax.broadcasted_iota(i32, (1, LANES), 1) // fgroup
    half_group = lax.rem(tile_group, per_tile // 2)
    low_half = lax.broadcasted_iota(i32, (1, LANES), 1) < half

    def pick(result, group, groups, height, lanes):
        picked = result[0:height, lanes]
        for g in range(1, groups):
            picked = jnp.where(group == g, result[g * height : (g + 1) * height, lanes], picked)
        return picked

    below = [lane[0:PACK] <= row[0:PACK] + r * PACK for r in range(BASE // PACK)]

    def prepare(ct):
        first = pl.multiple_of(ct * per_tile, per_tile)
        filt = rev[pl.ds(first, per_tile), :]
        zero = jnp.zeros((PACK, LANES), bf16)
        near = []
        for g in range(per_tile):
            ring = []
            for d in range(REACH):
                line = jnp.broadcast_to(filt[g : g + 1, d * LANES : (d + 1) * LANES], (PACK, LANES))
                ring.append(pltpu.roll(line, 0, 1, stride=1, stride_axis=0).astype(bf16))
            for r in range(BASE // PACK):
                turned = ring if r == 0 else [pltpu.roll(c, r * PACK, 1) for c in ring]
                at_row = g * BASE + r * PACK
                for w in range(REACH):
                    d = REACH - w
                    recent = turned[d] if d < REACH else zero
                    taps[ct, w, at_row : at_row + PACK, :] = jnp.where(below[r], recent, turned[d - 1])
            for r in range(half // PACK):
                turned = ring[0] if r == 0 else pltpu.roll(ring[0], r * PACK, 1)
                at_mask = slice(r * PACK, (r + 1) * PACK)
                near.append(jnp.concatenate([turned * near_mask[0, at_mask], turned * near_mask[1, at_mask]], 1))
        block = own[ct]
        first_half, second_half = block[:half], block[half:]
        none = jnp.zeros((half, LANES), bf16)
        right = jnp.concatenate(
            [
                jnp.concatenate([first_half, none, none, none], 0),
                jnp.concatenate([none, first_half, second_half, none], 0),
            ],
            1,
        )
        result = jnp.dot(jnp.concatenate(near, 0), right, preferred_element_type=f32)
        acc[ct, 0:half, :] = pick(result, tile_group, per_tile, half, slice(0, LANES))
        acc[ct, half:, :] = pick(result, tile_group, per_tile, half, slice(LANES, 2 * LANES))

    slots = []
    for w in range(REACH):
        q = lax.rem(at + w, REACH)
        slots.append(lax.rem(q // 2 + upper, 2) * 2 + lax.rem(q + at, 2))

    def far(ct):
        left = jnp.concatenate([got[slots[w], ct] * far_mask[w] for w in range(REACH)], 0)
        gap = jnp.zeros((BASE, LANES), bf16)
        later = jnp.concatenate([left[BASE:], gap], 0)
        outs = []
        for h in range(2):
            if h == 0:
                pair = jnp.where(low_half, left, pltpu.roll(later, half, 1))
            else:
                pair = jnp.where(low_half, pltpu.roll(left, half, 1), later)
            wide = jnp.concatenate([pair, jnp.concatenate([pair[2 * BASE :], gap, gap], 0)], 1)
            height = per_tile // 2 * BASE
            lhs = jnp.concatenate([taps[ct, w, h * height : (h + 1) * height, :] for w in range(REACH)], 1)
            result = jnp.dot(lhs, wide, preferred_element_type=f32)
            outs.append(
                [pick(result, half_group, per_tile // 2, BASE, slice(p * LANES, (p + 1) * LANES)) for p in range(2)]
            )
        both = []
        for p in range(2):
            both.append(jnp.where(low_half, outs[0][p], pltpu.roll(outs[1][p], half, 1)))
            both.append(jnp.where(low_half, pltpu.roll(outs[0][p], half, 1), outs[1][p]))
        total = acc[ct] + jnp.concatenate(both, 0) * out_mask[...]
        out_ref[:, lanes_of(ct)] = (gl_ref[:, lanes_of(ct)].astype(f32) * total).astype(bf16)

    def step(s, _):
        @pl.when(s < MSGS)
        def _():
            for u in range(each):
                prepare(s * each + u)

            def relay(copy):
                pl.when(has_prev)(lambda: copy(0, None, core_mate).wait_recv())
                pl.when(upper == 1)(lambda: copy(2, 0, row_mate).start())
                pl.when(core == 1)(lambda: copy(1, 0, core_mate).start())

            pl.when(s == EARLY)(lambda: relay(head_copy))
            relay(msg(s))

        @pl.when((s >= LAG1) & (s < MSGS + LAG1))
        def _():
            def relay(copy):
                copy(2, None, core_mate).wait_recv()
                copy(3, 2, core_mate).start()

            pl.when(s == EARLY + LAG1)(lambda: relay(head_copy))
            relay(msg(s - LAG1))

        @pl.when(s >= LAG2)
        def _():
            def arrive(copy):
                copy(1, None, core_mate).wait_recv()
                copy(3, None, core_mate).wait_recv()

            pl.when(s == LAG2)(lambda: arrive(head_copy))
            arrive(msg(s - LAG2))
            for u in range(each):
                far((s - LAG2) * each + u)

        return 0

    lax.fori_loop(0, MSGS + LAG2, step, 0)

    def drain_all(copy):
        pl.when(has_next)(lambda: copy(0, None, core_mate).wait_send())
        for slot in (1, 2, 3):
            copy(slot, None, core_mate).wait_send()

    def drain(j, _):
        drain_all(msg(j))
        return 0

    lax.fori_loop(0, MSGS, drain, 0)
    drain_all(head_copy)
    pl.when(me + 1 < count)(lambda: rim_copy(core_mate).wait_send())
    for d in range(1, REACH + 1):
        pl.when(me + d < count)(lambda d=d: doc_copy(d, core_mate).wait_send())


def body(gate_short, key_short, value_short, gate_long, doc_ids, se_filter, long_filter):
    rows, chans = gate_short.shape
    tap_count, filters = se_filter.shape
    fgroup = chans // filters
    count = lax.axis_size("ctx")
    tiles = chans // LANES
    assert rows * REACH == MAXDOC and rows == LANES and count % REACH == 0
    assert tap_count <= RIM and LANES % fgroup == 0 and filters % LANES == 0
    assert tiles % MSGS == 0 and tiles % 4 == 0 and long_filter.shape[1] == MAXDOC
    bf16, f32 = jnp.bfloat16, jnp.float32
    anywhere = pl.BlockSpec(memory_space=pl.ANY)
    dma = pltpu.SemaphoreType.DMA
    return pl.pallas_call(
        functools.partial(kernel, count),
        out_shape=jax.ShapeDtypeStruct((rows, chans), bf16),
        in_specs=[anywhere] * 7,
        out_specs=pl.BlockSpec(memory_space=pltpu.VMEM),
        scratch_shapes=[
            pltpu.VMEM((rows, chans), bf16),
            pltpu.VMEM((rows, chans), bf16),
            pltpu.VMEM((rows, chans), bf16),
            pltpu.VMEM((rows, chans), bf16),
            pltpu.VMEM((1, rows), jnp.int32),
            pltpu.VMEM((tap_count, filters), f32),
            pltpu.VMEM((filters, MAXDOC), bf16),
            pltpu.VMEM((RIM, chans), bf16),
            pltpu.VMEM((RIM, chans), bf16),
            pltpu.VMEM((tiles, rows, LANES), bf16),
            pltpu.VMEM((REACH, tiles, rows, LANES), bf16),
            pltpu.VMEM((8, LANES), f32),
            pltpu.VMEM((REACH, 8, LANES), f32),
            pltpu.VMEM((RIM, chans), bf16),
            pltpu.VMEM((RIM, chans), bf16),
            pltpu.VMEM((filters // LANES, 8, LANES), f32),
            pltpu.VMEM((RIM + rows, LANES), f32),
            pltpu.VMEM((max(4, tiles // MSGS), RIM + rows, LANES), f32),
            pltpu.VMEM((tap_count, rows, LANES), f32),
            pltpu.VMEM((filters, MAXDOC), f32),
            pltpu.VMEM((tiles, REACH, LANES // fgroup * BASE, LANES), bf16),
            pltpu.VMEM((tiles, rows, LANES), f32),
            pltpu.VMEM((2, rows // 2, LANES), bf16),
            pltpu.VMEM((REACH, rows, LANES), bf16),
            pltpu.VMEM((rows, LANES), f32),
            dma((3, MSGS)),
            dma((6,)),
            dma((REACH, MSGS)),
            dma((REACH, MSGS)),
            dma((REACH,)),
            dma((REACH,)),
            dma((REACH,)),
            dma((REACH,)),
            dma,
            dma,
        ],
        compiler_params=pltpu.CompilerParams(
            collective_id=0, has_side_effects=True, vmem_limit_bytes=40 * 1024 * 1024
        ),
    )(gate_short, key_short, value_short, gate_long, doc_ids.reshape(1, rows), se_filter, long_filter)


def solution(mesh):
    placed = P(("groups", "ctx"), None)
    return jax.shard_map(
        body,
        mesh=mesh,
        in_specs=(placed, placed, placed, placed, P(("groups", "ctx")), P(), P()),
        out_specs=placed,
        check_vma=False,
    )
```

```python
import functools

import jax
import jax.numpy as jnp
from jax import lax
from jax.experimental import pallas as pl
from jax.experimental.pallas import tpu as pltpu
from jax.sharding import PartitionSpec as P

MAXDOC = 512
REACH = 4
RIM = 8
LANES = 128
PACK = 16
MSGS = 16
EARLY = 3
LAG1 = 2
LAG2 = 6
BASE = 32
MESH = pl.DeviceIdType.MESH


def kernel(
    count, gs_hbm, k_hbm, v_hbm, gl_hbm, doc_hbm, se_hbm, h_hbm, out_ref,
    gs_ref, k_ref, v_ref, gl_ref, doc_ref, se_ref, h_ref, tail_k, tail_v,
    own, got, doc_out, got_doc, rim_out, rim_in, se_two, doc_ext, ext, agree,
    rev, taps, acc, near_mask, far_mask, out_mask, ring_all,
    in_sem, one_sem, send_sem, recv_sem, head_send, head_recv, doc_send, doc_recv, rim_send, rim_recv,
):
    rows, chans = gs_ref.shape
    tap_count, filters = se_ref.shape
    fgroup = chans // filters
    per_tile = LANES // fgroup
    tiles = chans // LANES
    each = tiles // MSGS
    width = each * LANES
    half = rows // 2
    body_rows = rows - RIM
    f32, bf16, i32 = jnp.float32, jnp.bfloat16, jnp.int32

    me = lax.axis_index("ctx")
    at = lax.rem(me, REACH)
    core = lax.rem(me, 2)
    upper = at // 2
    core_mate = me + 1 - 2 * core
    row_mate = me + 2 - 4 * upper
    has_prev = me >= REACH
    has_next = me + REACH < count
    core_filled = has_prev | (core == 1)
    row_filled = has_prev | (upper == 1)

    def local(src, dst, sem):
        return pltpu.make_async_copy(src, dst, sem)

    def piece(i, j):
        src, dst = ((k_hbm, k_ref), (v_hbm, v_ref), (gs_hbm, gs_ref))[i]
        cols = pl.ds(pl.multiple_of(j * width, width), width)
        return local(src.at[:, cols], dst.at[:, cols], in_sem.at[i, j])

    doc_in = local(doc_hbm, doc_ref, one_sem.at[0])
    tails = [
        local(k_hbm.at[pl.ds(rows - RIM, RIM), :], tail_k, one_sem.at[1]),
        local(v_hbm.at[pl.ds(rows - RIM, RIM), :], tail_v, one_sem.at[2]),
    ]
    se_in = local(se_hbm, se_ref, one_sem.at[3])
    h_in = local(h_hbm, h_ref, one_sem.at[4])
    gl_in = local(gl_hbm, gl_ref, one_sem.at[5])

    for i in range(2):
        piece(i, 0).start()
    se_in.start()
    piece(2, 0).start()
    doc_in.start()
    tails[0].start()
    tails[1].start()

    barrier = pltpu.get_barrier_semaphore()

    def greet(target):
        pl.semaphore_signal(barrier, inc=1, device_id={"ctx": target}, device_id_type=MESH)

    peers = jnp.int32(0)
    for d in range(1, REACH + 1):
        pl.when(me >= d)(lambda d=d: greet(me - d))
        pl.when(me + d < count)(lambda d=d: greet(me + d))
        peers = peers + (me >= d).astype(i32) + (me + d < count).astype(i32)

    def fetch(j, _):
        for i in range(3):
            piece(i, j).start()
        return 0

    lax.fori_loop(1, MSGS, fetch, 0)
    h_in.start()
    gl_in.start()

    lane = lax.broadcasted_iota(i32, (rows, LANES), 1)
    row = lax.broadcasted_iota(i32, (rows, LANES), 0)

    doc_in.wait()
    doc_row = jnp.broadcast_to(doc_ref[...].astype(f32), (rows, LANES))
    doc_col = doc_row.T
    doc_out[...] = doc_row[0:8]
    doc_ext[RIM:, :] = doc_col
    tails[0].wait()
    tails[1].wait()
    rim_out[...] = (tail_k[...].astype(f32) * tail_v[...].astype(f32)).astype(bf16)

    def remote(src, dst, ssem, rsem, target):
        return pltpu.make_async_remote_copy(
            src_ref=src, dst_ref=dst, send_sem=ssem, recv_sem=rsem,
            device_id={"ctx": target}, device_id_type=MESH,
        )

    def rim_copy(target):
        return remote(rim_out, rim_in, rim_send, rim_recv, target)

    def doc_copy(d, target):
        slot = REACH - d
        return remote(doc_out, got_doc.at[slot], doc_send.at[slot], doc_recv.at[slot], target)

    def msg_copy(slot, m, source, target):
        block = own if source is None else got.at[source]
        part = (pl.ds(m * each, each), pl.ds(RIM, body_rows))
        return remote(block.at[part], got.at[(slot, *part)], send_sem.at[slot, m], recv_sem.at[slot, m], target)

    def head_copy(slot, source, target):
        block = own if source is None else got.at[source]
        part = (pl.ds(0, tiles), pl.ds(0, RIM))
        return remote(block.at[part], got.at[(slot, *part)], head_send.at[slot], head_recv.at[slot], target)

    def send_own(copy):
        pl.when(has_next)(lambda: copy(0, None, me + REACH).start())
        pl.when(upper == 0)(lambda: copy(2, None, row_mate).start())
        pl.when(core == 0)(lambda: copy(1, None, core_mate).start())

    def msg(m):
        return lambda slot, source, target: msg_copy(slot, m, source, target)

    for tap in range(1, tap_count):
        agree[tap, RIM:, :] = (doc_ext[2 * RIM - tap : RIM + rows - tap, :] == doc_col[RIM:]).astype(f32)

    se_in.wait()
    for part in range(filters // LANES):
        se_two[part, 0:tap_count, :] = se_ref[:, part * LANES : (part + 1) * LANES]
        se_two[part, tap_count:, :] = jnp.zeros((8 - tap_count, LANES), f32)

    tiles_per_part = LANES // per_tile
    spread = lax.broadcasted_iota(i32, (8, LANES), 1) // fgroup

    def weights_of(ct):
        index = spread + lax.rem(ct, tiles_per_part) * per_tile
        return jnp.take_along_axis(se_two[ct // tiles_per_part], index, axis=1)

    def lanes_of(ct):
        return pl.ds(pl.multiple_of(ct * LANES, LANES), LANES)

    def product(ct, part):
        lanes = lanes_of(ct)
        return (k_ref[part, lanes].astype(f32) * v_ref[part, lanes].astype(f32)).astype(bf16).astype(f32)

    def await_piece(j, _):
        for i in range(3):
            piece(i, j).wait()
        return 0

    def short_body(j, _):
        for u in range(each):
            ct = j * each + u
            weights = weights_of(ct)
            kv = product(ct, slice(None))
            ext[u, RIM:, :] = kv
            total = kv[RIM:] * weights[0:1, :]
            for tap in range(1, tap_count):
                shifted = ext[u, 2 * RIM - tap : RIM + rows - tap, :]
                total = total + (shifted * agree[tap, RIM:, :]) * weights[tap : tap + 1, :]
            mixed = gs_ref[RIM:, lanes_of(ct)].astype(f32) * total
            own[ct, RIM:, :] = mixed.astype(bf16)
        return 0

    def early_body(j, _):
        await_piece(j, 0)
        return short_body(j, 0)

    lax.fori_loop(0, EARLY, early_body, 0)

    pl.semaphore_wait(barrier, peers)
    pl.when(me + 1 < count)(lambda: rim_copy(me + 1).start())
    for d in range(1, REACH + 1):
        pl.when(me + d < count)(lambda d=d: doc_copy(d, me + d).start())

    def send_msg(j, _):
        send_own(msg(j))
        return 0

    lax.fori_loop(0, EARLY, send_msg, 0)


    def clear(slot):
        got[slot] = jnp.zeros(got.shape[1:], bf16)

    @pl.when(jnp.logical_not(has_prev))
    def _():
        clear(0)
        pl.when(core == 0)(lambda: clear(1))
        pl.when(upper == 0)(lambda: clear(2))
        pl.when(upper == 0)(lambda: clear(3))

    h_in.wait()
    lag = lax.broadcasted_iota(i32, (LANES, LANES), 0)
    pos = lax.broadcasted_iota(i32, (LANES, LANES), 1)
    flip = jnp.where(lag == lax.rem(LANES - pos, LANES), 1.0, 0.0).astype(bf16)
    for d in range(REACH):
        cols = slice(d * LANES, (d + 1) * LANES)
        rev[:, cols] = jnp.dot(h_ref[:, cols], flip, preferred_element_type=f32)

    low = lane[:half] < half
    causal = lane[:half] <= row[:half]
    same_low = doc_col[:half] == doc_row[:half]
    same_high = doc_col[half:] == pltpu.roll(doc_row[:half], half, 1)
    late = same_high.astype(f32)
    early = causal.astype(f32) * same_low.astype(f32)
    near_mask[0] = jnp.where(low, early, late).astype(bf16)
    near_mask[1] = jnp.where(low, causal.astype(f32) * late, 0.0).astype(bf16)
    leader = jnp.broadcast_to(doc_row[0:1, 0:1], (rows, LANES))
    out_mask[...] = (doc_col == leader).astype(f32)

    for w in range(REACH):
        pl.when(me >= REACH - w)(lambda w=w: doc_copy(REACH - w, core_mate).wait_recv())

        @pl.when(me < REACH - w)
        def _():
            got_doc[w] = jnp.full((8, LANES), -1.0, f32)

        source_col = jnp.broadcast_to(got_doc[w, 0:1, :], (rows, LANES)).T
        far_mask[w] = (source_col == leader).astype(bf16)
        if w == REACH - 1:
            doc_ext[0:RIM, :] = source_col[rows - RIM :]

    @pl.when(me == 0)
    def _():
        rim_in[...] = jnp.zeros((RIM, chans), bf16)

    @pl.when(me > 0)
    def _():
        rim_copy(core_mate).wait_recv()

    for tap in range(1, tap_count):
        agree[tap, 0:RIM, :] = (doc_ext[RIM - tap : 2 * RIM - tap, :] == doc_col[0:RIM]).astype(f32)

    lax.fori_loop(EARLY, MSGS, await_piece, 0)

    def short_head(j, _):
        for u in range(4):
            ct = j * 4 + u
            weights = weights_of(ct)
            kv = product(ct, slice(0, RIM))
            ext[u, 0:RIM, :] = rim_in[:, lanes_of(ct)].astype(f32)
            ext[u, RIM : 2 * RIM, :] = kv
            total = kv * weights[0:1, :]
            for tap in range(1, tap_count):
                shifted = ext[u, RIM - tap : 2 * RIM - tap, :]
                total = total + (shifted * agree[tap, 0:RIM, :]) * weights[tap : tap + 1, :]
            mixed = gs_ref[0:RIM, lanes_of(ct)].astype(f32) * total
            own[ct, 0:RIM, :] = mixed.astype(bf16)
        return 0

    lax.fori_loop(0, tiles // 4, short_head, 0)
    send_own(head_copy)

    gl_in.wait()

    tile_group = lax.broadcasted_iota(i32, (1, LANES), 1) // fgroup
    half_group = lax.rem(tile_group, per_tile // 2)
    low_half = lax.broadcasted_iota(i32, (1, LANES), 1) < half

    def pick(result, group, groups, height, lanes):
        picked = result[0:height, lanes]
        for g in range(1, groups):
            picked = jnp.where(group == g, result[g * height : (g + 1) * height, lanes], picked)
        return picked

    below = [lane[0:PACK] <= row[0:PACK] + r * PACK for r in range(BASE // PACK)]

    def prepare(ct, ring_rows):
        first = pl.multiple_of(ct * per_tile, per_tile)
        filt = rev[pl.ds(first, per_tile), :]
        for d in range(REACH):
            line = filt[:, d * LANES : (d + 1) * LANES]
            for i in range(PACK):
                ring_rows[d, pl.ds(i, per_tile, stride=PACK), :] = line if i == 0 else pltpu.roll(line, i, 1)
        zero = jnp.zeros((PACK, LANES), bf16)
        near = []
        for g in range(per_tile):
            ring = [ring_rows[d, g * PACK : (g + 1) * PACK, :].astype(bf16) for d in range(REACH)]
            for r in range(BASE // PACK):
                turned = ring if r == 0 else [pltpu.roll(c, r * PACK, 1) for c in ring]
                at_row = g * BASE + r * PACK
                for w in range(REACH):
                    d = REACH - w
                    recent = turned[d] if d < REACH else zero
                    taps[ct, w, at_row : at_row + PACK, :] = jnp.where(below[r], recent, turned[d - 1])
            for r in range(half // PACK):
                turned = ring[0] if r == 0 else pltpu.roll(ring[0], r * PACK, 1)
                at_mask = slice(r * PACK, (r + 1) * PACK)
                near.append(jnp.concatenate([turned * near_mask[0, at_mask], turned * near_mask[1, at_mask]], 1))
        block = own[ct]
        first_half, second_half = block[:half], block[half:]
        none = jnp.zeros((half, LANES), bf16)
        right = jnp.concatenate(
            [
                jnp.concatenate([first_half, none, none, none], 0),
                jnp.concatenate([none, first_half, second_half, none], 0),
            ],
            1,
        )
        result = jnp.dot(jnp.concatenate(near, 0), right, preferred_element_type=f32)
        acc[ct, 0:half, :] = pick(result, tile_group, per_tile, half, slice(0, LANES))
        acc[ct, half:, :] = pick(result, tile_group, per_tile, half, slice(LANES, 2 * LANES))

    slots = []
    for w in range(REACH):
        q = lax.rem(at + w, REACH)
        slots.append(lax.rem(q // 2 + upper, 2) * 2 + lax.rem(q + at, 2))

    def far(ct):
        left = jnp.concatenate([got[slots[w], ct] * far_mask[w] for w in range(REACH)], 0)
        gap = jnp.zeros((BASE, LANES), bf16)
        later = jnp.concatenate([left[BASE:], gap], 0)
        outs = []
        for h in range(2):
            if h == 0:
                pair = jnp.where(low_half, left, pltpu.roll(later, half, 1))
            else:
                pair = jnp.where(low_half, pltpu.roll(left, half, 1), later)
            wide = jnp.concatenate([pair, jnp.concatenate([pair[2 * BASE :], gap, gap], 0)], 1)
            height = per_tile // 2 * BASE
            lhs = jnp.concatenate([taps[ct, w, h * height : (h + 1) * height, :] for w in range(REACH)], 1)
            result = jnp.dot(lhs, wide, preferred_element_type=f32)
            outs.append(
                [pick(result, half_group, per_tile // 2, BASE, slice(p * LANES, (p + 1) * LANES)) for p in range(2)]
            )
        both = []
        for p in range(2):
            both.append(jnp.where(low_half, outs[0][p], pltpu.roll(outs[1][p], half, 1)))
            both.append(jnp.where(low_half, pltpu.roll(outs[0][p], half, 1), outs[1][p]))
        total = acc[ct] + jnp.concatenate(both, 0) * out_mask[...]
        out_ref[:, lanes_of(ct)] = (gl_ref[:, lanes_of(ct)].astype(f32) * total).astype(bf16)

    def step(s, _):
        @pl.when(s < MSGS - EARLY)
        def _():
            short_body(s + EARLY, 0)
            send_own(msg(s + EARLY))

        @pl.when(s < MSGS)
        def _():
            for u in range(each):
                prepare(s * each + u, ring_all.at[u])

            def relay(copy):
                pl.when(has_prev)(lambda: copy(0, None, core_mate).wait_recv())
                pl.when(has_prev & (upper == 1))(lambda: copy(2, 0, row_mate).start())
                pl.when(has_prev & (core == 1))(lambda: copy(1, 0, core_mate).start())

            pl.when(s == EARLY)(lambda: relay(head_copy))
            relay(msg(s))

        @pl.when((s >= LAG1) & (s < MSGS + LAG1))
        def _():
            def relay(copy):
                pl.when(row_filled)(lambda: copy(2, None, core_mate).wait_recv())
                pl.when(row_filled)(lambda: copy(3, 2, core_mate).start())

            pl.when(s == EARLY + LAG1)(lambda: relay(head_copy))
            relay(msg(s - LAG1))

        @pl.when(s >= LAG2)
        def _():
            def arrive(copy):
                pl.when(core_filled)(lambda: copy(1, None, core_mate).wait_recv())
                pl.when(row_filled)(lambda: copy(3, None, core_mate).wait_recv())

            pl.when(s == LAG2)(lambda: arrive(head_copy))
            arrive(msg(s - LAG2))
            for u in range(each):
                far((s - LAG2) * each + u)

        return 0

    lax.fori_loop(0, MSGS + LAG2, step, 0)

    def drain_all(copy):
        pl.when(has_next)(lambda: copy(0, None, core_mate).wait_send())
        pl.when(has_prev | (core == 0))(lambda: copy(1, None, core_mate).wait_send())
        pl.when(has_prev | (upper == 0))(lambda: copy(2, None, core_mate).wait_send())
        pl.when(row_filled)(lambda: copy(3, None, core_mate).wait_send())

    def drain(j, _):
        drain_all(msg(j))
        return 0

    lax.fori_loop(0, MSGS, drain, 0)
    drain_all(head_copy)
    pl.when(me + 1 < count)(lambda: rim_copy(core_mate).wait_send())
    for d in range(1, REACH + 1):
        pl.when(me + d < count)(lambda d=d: doc_copy(d, core_mate).wait_send())


def body(gate_short, key_short, value_short, gate_long, doc_ids, se_filter, long_filter):
    rows, chans = gate_short.shape
    tap_count, filters = se_filter.shape
    fgroup = chans // filters
    count = lax.axis_size("ctx")
    tiles = chans // LANES
    assert rows * REACH == MAXDOC and rows == LANES and count % REACH == 0
    assert tap_count <= RIM and LANES % fgroup == 0 and filters % LANES == 0
    assert tiles % MSGS == 0 and tiles % 4 == 0 and long_filter.shape[1] == MAXDOC
    bf16, f32 = jnp.bfloat16, jnp.float32
    anywhere = pl.BlockSpec(memory_space=pl.ANY)
    dma = pltpu.SemaphoreType.DMA
    return pl.pallas_call(
        functools.partial(kernel, count),
        out_shape=pltpu.VMEM((rows, chans), bf16),
        in_specs=[anywhere] * 7,
        out_specs=pl.BlockSpec(memory_space=pltpu.VMEM),
        scratch_shapes=[
            pltpu.VMEM((rows, chans), bf16),
            pltpu.VMEM((rows, chans), bf16),
            pltpu.VMEM((rows, chans), bf16),
            pltpu.VMEM((rows, chans), bf16),
            pltpu.VMEM((1, rows), jnp.int32),
            pltpu.VMEM((tap_count, filters), f32),
            pltpu.VMEM((filters, MAXDOC), bf16),
            pltpu.VMEM((RIM, chans), bf16),
            pltpu.VMEM((RIM, chans), bf16),
            pltpu.VMEM((tiles, rows, LANES), bf16),
            pltpu.VMEM((REACH, tiles, rows, LANES), bf16),
            pltpu.VMEM((8, LANES), f32),
            pltpu.VMEM((REACH, 8, LANES), f32),
            pltpu.VMEM((RIM, chans), bf16),
            pltpu.VMEM((RIM, chans), bf16),
            pltpu.VMEM((filters // LANES, 8, LANES), f32),
            pltpu.VMEM((RIM + rows, LANES), f32),
            pltpu.VMEM((max(4, tiles // MSGS), RIM + rows, LANES), f32),
            pltpu.VMEM((tap_count, rows, LANES), f32),
            pltpu.VMEM((filters, MAXDOC), f32),
            pltpu.VMEM((tiles, REACH, LANES // fgroup * BASE, LANES), bf16),
            pltpu.VMEM((tiles, rows, LANES), f32),
            pltpu.VMEM((2, rows // 2, LANES), bf16),
            pltpu.VMEM((REACH, rows, LANES), bf16),
            pltpu.VMEM((rows, LANES), f32),
            pltpu.VMEM((tiles // MSGS, REACH, LANES // fgroup * PACK, LANES), f32),
            dma((3, MSGS)),
            dma((6,)),
            dma((REACH, MSGS)),
            dma((REACH, MSGS)),
            dma((REACH,)),
            dma((REACH,)),
            dma((REACH,)),
            dma((REACH,)),
            dma,
            dma,
        ],
        compiler_params=pltpu.CompilerParams(
            collective_id=0, has_side_effects=True, vmem_limit_bytes=48 * 1024 * 1024
        ),
    )(*(
        pltpu.with_memory_space_constraint(x, pltpu.HBM)
        for x in (gate_short, key_short, value_short, gate_long, doc_ids.reshape(1, rows), se_filter, long_filter)
    ))


def solution(mesh):
    placed = P(("groups", "ctx"), None)
    return jax.shard_map(
        body,
        mesh=mesh,
        in_specs=(placed, placed, placed, placed, P(("groups", "ctx")), P(), P()),
        out_specs=placed,
        check_vma=False,
    )
```

```python
import functools

import jax
import jax.numpy as jnp
from jax import lax
from jax.experimental import pallas as pl
from jax.experimental.pallas import tpu as pltpu
from jax.sharding import PartitionSpec as P

MAXDOC = 512
REACH = 4
RIM = 8
LANES = 128
PACK = 16
MSGS = 16
EARLY = 3
LAG1 = 2
LAG2 = 4
VIA = 2
BASE = 32
MESH = pl.DeviceIdType.MESH


def kernel(
    count, gs_hbm, k_hbm, v_hbm, gl_hbm, doc_hbm, se_hbm, h_hbm, out_ref,
    gs_ref, k_ref, v_ref, gl_ref, doc_ref, se_ref, h_ref, tail_k, tail_v,
    own, got, doc_out, got_doc, rim_out, rim_in, se_two, doc_ext, ext, agree,
    rev, taps, acc, near_mask, pair_mask, out_mask, doc_all, ring_all, via,
    in_sem, one_sem, send_sem, recv_sem, head_send, head_recv, doc_send, doc_recv, rim_send, rim_recv,
    via_send, via_recv, fwd_send,
):
    rows, chans = gs_ref.shape
    tap_count, filters = se_ref.shape
    fgroup = chans // filters
    per_tile = LANES // fgroup
    tiles = chans // LANES
    each = tiles // MSGS
    width = each * LANES
    half = rows // 2
    direct = MSGS - VIA
    body_rows = rows - RIM
    f32, bf16, i32 = jnp.float32, jnp.bfloat16, jnp.int32

    me = lax.axis_index("ctx")
    at = lax.rem(me, REACH)
    core = lax.rem(me, 2)
    upper = at // 2
    core_mate = me + 1 - 2 * core
    row_mate = me + 2 - 4 * upper
    has_prev = me >= REACH
    has_next = me + REACH < count
    core_filled = has_prev | (core == 1)
    row_filled = has_prev | (upper == 1)

    def local(src, dst, sem):
        return pltpu.make_async_copy(src, dst, sem)

    def piece(i, j):
        src, dst = ((k_hbm, k_ref), (v_hbm, v_ref), (gs_hbm, gs_ref))[i]
        cols = pl.ds(pl.multiple_of(j * width, width), width)
        return local(src.at[:, cols], dst.at[:, cols], in_sem.at[i, j])

    doc_in = local(doc_hbm, doc_ref, one_sem.at[0])
    tails = [
        local(k_hbm.at[pl.ds(rows - RIM, RIM), :], tail_k, one_sem.at[1]),
        local(v_hbm.at[pl.ds(rows - RIM, RIM), :], tail_v, one_sem.at[2]),
    ]
    se_in = local(se_hbm, se_ref, one_sem.at[3])
    h_in = local(h_hbm, h_ref, one_sem.at[4])
    gl_in = local(gl_hbm, gl_ref, one_sem.at[5])

    for i in range(2):
        piece(i, 0).start()
    se_in.start()
    piece(2, 0).start()
    doc_in.start()
    tails[0].start()
    tails[1].start()

    barrier = pltpu.get_barrier_semaphore()

    def greet(target):
        pl.semaphore_signal(barrier, inc=1, device_id={"ctx": target}, device_id_type=MESH)

    peers = jnp.int32(0)
    for d in range(1, REACH + 1):
        pl.when(me >= d)(lambda d=d: greet(me - d))
        pl.when(me + d < count)(lambda d=d: greet(me + d))
        peers = peers + (me >= d).astype(i32) + (me + d < count).astype(i32)

    def fetch(j, _):
        for i in range(3):
            piece(i, j).start()
        return 0

    lax.fori_loop(1, MSGS, fetch, 0)
    h_in.start()
    gl_in.start()

    lane = lax.broadcasted_iota(i32, (rows, LANES), 1)
    row = lax.broadcasted_iota(i32, (rows, LANES), 0)

    doc_in.wait()
    doc_row = jnp.broadcast_to(doc_ref[...].astype(f32), (rows, LANES))
    doc_col = doc_row.T
    doc_out[...] = doc_row[0:8]
    doc_ext[RIM:, :] = doc_col
    tails[0].wait()
    tails[1].wait()
    rim_out[...] = (tail_k[...].astype(f32) * tail_v[...].astype(f32)).astype(bf16)

    def remote(src, dst, ssem, rsem, target):
        return pltpu.make_async_remote_copy(
            src_ref=src, dst_ref=dst, send_sem=ssem, recv_sem=rsem,
            device_id={"ctx": target}, device_id_type=MESH,
        )

    def rim_copy(target):
        return remote(rim_out, rim_in, rim_send, rim_recv, target)

    def doc_copy(d, target):
        slot = REACH - d
        return remote(doc_out, got_doc.at[slot], doc_send.at[slot], doc_recv.at[slot], target)

    def msg_copy(slot, m, source, target):
        block = own if source is None else got.at[source]
        part = (pl.ds(m * each, each), pl.ds(RIM, body_rows))
        return remote(block.at[part], got.at[(slot, *part)], send_sem.at[slot, m], recv_sem.at[slot, m], target)

    def head_copy(slot, source, target):
        block = own if source is None else got.at[source]
        part = (pl.ds(0, tiles), pl.ds(0, RIM))
        return remote(block.at[part], got.at[(slot, *part)], head_send.at[slot], head_recv.at[slot], target)

    def send_own(copy):
        pl.when(has_next)(lambda: copy(0, None, me + REACH).start())
        pl.when(upper == 0)(lambda: copy(2, None, row_mate).start())
        pl.when(core == 0)(lambda: copy(1, None, core_mate).start())

    def msg(m):
        return lambda slot, source, target: msg_copy(slot, m, source, target)

    for tap in range(1, tap_count):
        agree[tap, RIM:, :] = (doc_ext[2 * RIM - tap : RIM + rows - tap, :] == doc_col[RIM:]).astype(f32)

    se_in.wait()
    for part in range(filters // LANES):
        se_two[part, 0:tap_count, :] = se_ref[:, part * LANES : (part + 1) * LANES]
        se_two[part, tap_count:, :] = jnp.zeros((8 - tap_count, LANES), f32)

    tiles_per_part = LANES // per_tile
    spread = lax.broadcasted_iota(i32, (8, LANES), 1) // fgroup

    def weights_of(ct):
        index = spread + lax.rem(ct, tiles_per_part) * per_tile
        return jnp.take_along_axis(se_two[ct // tiles_per_part], index, axis=1)

    def lanes_of(ct):
        return pl.ds(pl.multiple_of(ct * LANES, LANES), LANES)

    def product(ct, part):
        lanes = lanes_of(ct)
        return (k_ref[part, lanes].astype(f32) * v_ref[part, lanes].astype(f32)).astype(bf16).astype(f32)

    def await_piece(j, _):
        for i in range(3):
            piece(i, j).wait()
        return 0

    def short_body(j, _):
        for u in range(each):
            ct = j * each + u
            weights = weights_of(ct)
            kv = product(ct, slice(None))
            ext[u, RIM:, :] = kv
            total = kv[RIM:] * weights[0:1, :]
            for tap in range(1, tap_count):
                shifted = ext[u, 2 * RIM - tap : RIM + rows - tap, :]
                total = total + (shifted * agree[tap, RIM:, :]) * weights[tap : tap + 1, :]
            mixed = gs_ref[RIM:, lanes_of(ct)].astype(f32) * total
            own[ct, RIM:, :] = mixed.astype(bf16)
        return 0

    def early_body(j, _):
        await_piece(j, 0)
        return short_body(j, 0)

    lax.fori_loop(0, EARLY, early_body, 0)
    lax.fori_loop(direct, MSGS, early_body, 0)

    pl.semaphore_wait(barrier, peers)
    pl.when(me + 1 < count)(lambda: rim_copy(me + 1).start())
    for d in range(1, REACH + 1):
        pl.when(me + d < count)(lambda d=d: doc_copy(d, me + d).start())

    def send_msg(j, _):
        send_own(msg(j))
        return 0

    def side(i):
        return pl.ds(i * each, each), pl.ds(RIM, body_rows)

    def via_copy(i, target):
        block = own.at[pl.ds((direct + i) * each, each), pl.ds(RIM, body_rows)]
        return remote(block, via.at[side(i)], via_send.at[i], via_recv.at[i], target)

    def fwd_copy(i, target):
        m = direct + i
        block = got.at[2, pl.ds(m * each, each), pl.ds(RIM, body_rows)]
        return remote(via.at[side(i)], block, fwd_send.at[i], recv_sem.at[2, m], target)

    for i in range(VIA):
        pl.when((upper == 1) & has_next)(lambda i=i: via_copy(i, row_mate).start())
    lax.fori_loop(0, EARLY, send_msg, 0)


    def clear(slot):
        got[slot] = jnp.zeros(got.shape[1:], bf16)

    @pl.when(jnp.logical_not(has_prev))
    def _():
        clear(0)
        pl.when(core == 0)(lambda: clear(1))
        pl.when(upper == 0)(lambda: clear(2))
        pl.when(upper == 0)(lambda: clear(3))

    h_in.wait()
    lag = lax.broadcasted_iota(i32, (LANES, LANES), 0)
    pos = lax.broadcasted_iota(i32, (LANES, LANES), 1)
    flip = jnp.where(lag == lax.rem(LANES - pos, LANES), 1.0, 0.0).astype(bf16)
    for d in range(REACH):
        cols = slice(d * LANES, (d + 1) * LANES)
        rev[:, cols] = jnp.dot(h_ref[:, cols], flip, preferred_element_type=f32)

    for w in range(REACH):
        pl.when(me >= REACH - w)(lambda w=w: doc_copy(REACH - w, core_mate).wait_recv())

        @pl.when(me < REACH - w)
        def _():
            got_doc[w] = jnp.full((8, LANES), -1.0, f32)

        source_col = jnp.broadcast_to(got_doc[w, 0:1, :], (rows, LANES)).T
        doc_all[w * rows : (w + 1) * rows, :] = source_col
        if w == REACH - 1:
            doc_ext[0:RIM, :] = source_col[rows - RIM :]
    doc_all[MAXDOC:, :] = doc_col

    windows = rows // BASE
    low = lane < half
    leaders = [jnp.broadcast_to(doc_col[a * BASE : a * BASE + 1, :], (MAXDOC, LANES)) for a in range(windows)]

    def matches(a):
        same = doc_all[a * BASE : a * BASE + MAXDOC, :] == leaders[a]
        return same.astype(f32)

    def matched(a):
        same = doc_col[a * BASE : (a + 1) * BASE] == leaders[a][:BASE]
        return same.astype(f32)

    low_tall = lax.broadcasted_iota(i32, (MAXDOC, LANES), 1) < half
    block_doc = doc_col[0:BASE]
    for a in range(1, windows):
        block_doc = jnp.where(lane[:BASE] // BASE == a, doc_col[a * BASE : (a + 1) * BASE], block_doc)
    causal = (lax.rem(lane[:BASE], BASE) <= row[:BASE]).astype(f32)
    near_mask[...] = (causal * (block_doc == doc_row[:BASE]).astype(f32)).astype(bf16)
    for p in range(windows // 2):
        pair_mask[p] = jnp.where(low_tall, matches(2 * p), matches(2 * p + 1)).astype(bf16)
        out_mask[p] = jnp.where(low[:BASE], matched(2 * p), matched(2 * p + 1))

    @pl.when(me == 0)
    def _():
        rim_in[...] = jnp.zeros((RIM, chans), bf16)

    @pl.when(me > 0)
    def _():
        rim_copy(core_mate).wait_recv()

    for tap in range(1, tap_count):
        agree[tap, 0:RIM, :] = (doc_ext[RIM - tap : 2 * RIM - tap, :] == doc_col[0:RIM]).astype(f32)

    lax.fori_loop(EARLY, direct, await_piece, 0)

    def short_head(j, _):
        for u in range(4):
            ct = j * 4 + u
            weights = weights_of(ct)
            kv = product(ct, slice(0, RIM))
            ext[u, 0:RIM, :] = rim_in[:, lanes_of(ct)].astype(f32)
            ext[u, RIM : 2 * RIM, :] = kv
            total = kv * weights[0:1, :]
            for tap in range(1, tap_count):
                shifted = ext[u, RIM - tap : 2 * RIM - tap, :]
                total = total + (shifted * agree[tap, 0:RIM, :]) * weights[tap : tap + 1, :]
            mixed = gs_ref[0:RIM, lanes_of(ct)].astype(f32) * total
            own[ct, 0:RIM, :] = mixed.astype(bf16)
        return 0

    lax.fori_loop(0, tiles // 4, short_head, 0)
    send_own(head_copy)

    @pl.when((upper == 0) & has_next)
    def _():
        for i in range(VIA):
            via_copy(i, row_mate).wait_recv()
            fwd_copy(i, me + REACH).start()

    gl_in.wait()

    tile_group = lax.broadcasted_iota(i32, (1, LANES), 1) // fgroup
    half_group = lax.rem(tile_group, per_tile // 2)
    low_half = lax.broadcasted_iota(i32, (1, LANES), 1) < half

    def pick(result, group, groups, height, lanes):
        picked = result[0:height, lanes]
        for g in range(1, groups):
            picked = jnp.where(group == g, result[g * height : (g + 1) * height, lanes], picked)
        return picked

    below = [lane[0:PACK] <= row[0:PACK] + r * PACK for r in range(BASE // PACK)]

    place = lax.rem(lane[0:PACK] + PACK, LANES) // BASE
    arc = [place == b for b in range(rows // BASE)]

    def prepare(ct, ring_rows):
        first = pl.multiple_of(ct * per_tile, per_tile)
        filt = rev[pl.ds(first, per_tile), :]
        for d in range(REACH):
            line = filt[:, d * LANES : (d + 1) * LANES]
            for i in range(PACK):
                ring_rows[d, pl.ds(i, per_tile, stride=PACK), :] = line if i == 0 else pltpu.roll(line, i, 1)
        zero = jnp.zeros((PACK, LANES), bf16)
        zero_base = jnp.zeros((BASE, LANES), bf16)
        near = []
        for g in range(per_tile):
            ring = [ring_rows[d, g * PACK : (g + 1) * PACK, :].astype(bf16) for d in range(REACH)]
            for r in range(BASE // PACK):
                turned = ring if r == 0 else [pltpu.roll(c, r * PACK, 1) for c in ring]
                at_row = g * BASE + r * PACK
                for w in range(REACH):
                    d = REACH - w
                    recent = turned[d] if d < REACH else zero
                    taps[ct, w, at_row : at_row + PACK, :] = jnp.where(below[r], recent, turned[d - 1])
            around = ring[0]
            for b in range(1, rows // BASE):
                around = jnp.where(arc[b], pltpu.roll(ring[0], b * BASE, 1), around)
            for r in range(BASE // PACK):
                turned = around if r == 0 else pltpu.roll(around, r * PACK, 1)
                near.append(turned * near_mask[r * PACK : (r + 1) * PACK])
        block = own[ct]
        turned = pltpu.roll(block, half, 1)
        none = jnp.zeros((half, LANES), bf16)
        for h in range(2):
            first, second = (block, turned) if h == 0 else (turned, block)
            spread_out = jnp.concatenate(
                [
                    jnp.where(low_half, first[a * BASE : (a + 1) * BASE], zero_base)
                    if a % 2 == 0
                    else jnp.where(low_half, zero_base, second[a * BASE : (a + 1) * BASE])
                    for a in range(rows // BASE)
                ],
                0,
            )
            right = jnp.concatenate(
                [jnp.concatenate([spread_out[:half], none], 0), jnp.concatenate([none, spread_out[half:]], 0)], 1
            )
            count_near = per_tile // 2 * (BASE // PACK)
            lhs = jnp.concatenate(near[h * count_near : (h + 1) * count_near], 0)
            result = jnp.dot(lhs, right, preferred_element_type=f32)
            for p in range(2):
                at_row = (2 * h + p) * BASE
                acc[ct, at_row : at_row + BASE, :] = pick(
                    result, half_group, per_tile // 2, BASE, slice(p * LANES, (p + 1) * LANES)
                )

    slots = []
    for w in range(REACH):
        q = lax.rem(at + w, REACH)
        slots.append(lax.rem(q // 2 + upper, 2) * 2 + lax.rem(q + at, 2))

    def far(ct):
        reach = [got[slots[w], ct] for w in range(REACH)] + [own[ct, 0 : rows - BASE, :]]
        source = jnp.concatenate(reach, 0)
        turned = pltpu.roll(source, half, 1)
        tall = MAXDOC + half
        outs = []
        for h in range(2):
            first, second = (source, turned) if h == 0 else (turned, source)
            pair = jnp.where(low_half, first[:tall], second[BASE : BASE + tall])
            wide = jnp.concatenate([pair[p * half : p * half + MAXDOC] * pair_mask[p] for p in range(2)], 1)
            height = per_tile // 2 * BASE
            lhs = jnp.concatenate([taps[ct, w, h * height : (h + 1) * height, :] for w in range(REACH)], 1)
            result = jnp.dot(lhs, wide, preferred_element_type=f32)
            total = []
            for p in range(2):
                picked = pick(result, half_group, per_tile // 2, BASE, slice(p * LANES, (p + 1) * LANES))
                at_row = (2 * h + p) * BASE
                total.append(acc[ct, at_row : at_row + BASE, :] + picked * out_mask[p])
            outs.append(total)
        both = []
        for p in range(2):
            both.append(jnp.where(low_half, outs[0][p], pltpu.roll(outs[1][p], half, 1)))
            both.append(jnp.where(low_half, pltpu.roll(outs[0][p], half, 1), outs[1][p]))
        total = jnp.concatenate(both, 0)
        out_ref[:, lanes_of(ct)] = (gl_ref[:, lanes_of(ct)].astype(f32) * total).astype(bf16)

    def step(s, _):
        @pl.when(s < MSGS - EARLY)
        def _():
            @pl.when(s < direct - EARLY)
            def _():
                short_body(s + EARLY, 0)

            send_own(msg(s + EARLY))

        def prepare_msg(m, _):
            for u in range(each):
                prepare(m * each + u, ring_all.at[u])
            return 0

        def prepared(s):
            return jnp.minimum(jnp.minimum(2 * s, s + EARLY), MSGS)

        lax.fori_loop(prepared(s), prepared(s + 1), prepare_msg, 0)

        @pl.when(s < MSGS)
        def _():
            def relay(copy, row_too=True):
                pl.when(has_prev)(lambda: copy(0, None, core_mate).wait_recv())
                pl.when(has_prev & (upper == 1) & row_too)(lambda: copy(2, 0, row_mate).start())
                pl.when(has_prev & (core == 1))(lambda: copy(1, 0, core_mate).start())

            pl.when(s == EARLY)(lambda: relay(head_copy))
            relay(msg(s), s < direct)

        @pl.when((s >= LAG1) & (s < MSGS + LAG1))
        def _():
            def relay(copy):
                pl.when(row_filled)(lambda: copy(2, None, core_mate).wait_recv())
                pl.when(row_filled)(lambda: copy(3, 2, core_mate).start())

            pl.when(s == EARLY + LAG1)(lambda: relay(head_copy))
            relay(msg(s - LAG1))

        def finished(s):
            ahead = jnp.maximum(s - (EARLY + LAG1 + 1), 0)
            return jnp.minimum(jnp.minimum(ahead + ahead // 3, jnp.maximum(s - LAG2, 0)), MSGS)

        def far_msg(m, _):
            def arrive(copy):
                pl.when(core_filled)(lambda: copy(1, None, core_mate).wait_recv())
                pl.when(row_filled)(lambda: copy(3, None, core_mate).wait_recv())

            pl.when(m == 0)(lambda: arrive(head_copy))
            arrive(msg(m))
            for u in range(each):
                far(m * each + u)
            return 0

        lax.fori_loop(finished(s), finished(s + 1), far_msg, 0)
        return 0

    lax.fori_loop(0, MSGS + LAG2, step, 0)

    def drain_all(copy, row_too=True):
        pl.when(has_next)(lambda: copy(0, None, core_mate).wait_send())
        pl.when(has_prev | (core == 0))(lambda: copy(1, None, core_mate).wait_send())
        pl.when((has_prev & row_too) | (upper == 0))(lambda: copy(2, None, core_mate).wait_send())
        pl.when(row_filled)(lambda: copy(3, None, core_mate).wait_send())

    def drain(j, _):
        drain_all(msg(j), j < direct)
        return 0

    lax.fori_loop(0, MSGS, drain, 0)
    drain_all(head_copy)
    for i in range(VIA):
        pl.when((upper == 1) & has_next)(lambda i=i: via_copy(i, core_mate).wait_send())
        pl.when((upper == 0) & has_next)(lambda i=i: fwd_copy(i, core_mate).wait_send())
    pl.when(me + 1 < count)(lambda: rim_copy(core_mate).wait_send())
    for d in range(1, REACH + 1):
        pl.when(me + d < count)(lambda d=d: doc_copy(d, core_mate).wait_send())


def body(gate_short, key_short, value_short, gate_long, doc_ids, se_filter, long_filter):
    rows, chans = gate_short.shape
    tap_count, filters = se_filter.shape
    fgroup = chans // filters
    count = lax.axis_size("ctx")
    tiles = chans // LANES
    assert rows * REACH == MAXDOC and rows == LANES and count % REACH == 0
    assert tap_count <= RIM and LANES % fgroup == 0 and filters % LANES == 0
    assert tiles % MSGS == 0 and tiles % 4 == 0 and long_filter.shape[1] == MAXDOC
    bf16, f32 = jnp.bfloat16, jnp.float32
    anywhere = pl.BlockSpec(memory_space=pl.ANY)
    dma = pltpu.SemaphoreType.DMA
    return pl.pallas_call(
        functools.partial(kernel, count),
        out_shape=pltpu.VMEM((rows, chans), bf16),
        in_specs=[anywhere] * 7,
        out_specs=pl.BlockSpec(memory_space=pltpu.VMEM),
        scratch_shapes=[
            pltpu.VMEM((rows, chans), bf16),
            pltpu.VMEM((rows, chans), bf16),
            pltpu.VMEM((rows, chans), bf16),
            pltpu.VMEM((rows, chans), bf16),
            pltpu.VMEM((1, rows), jnp.int32),
            pltpu.VMEM((tap_count, filters), f32),
            pltpu.VMEM((filters, MAXDOC), bf16),
            pltpu.VMEM((RIM, chans), bf16),
            pltpu.VMEM((RIM, chans), bf16),
            pltpu.VMEM((tiles, rows, LANES), bf16),
            pltpu.VMEM((REACH, tiles, rows, LANES), bf16),
            pltpu.VMEM((8, LANES), f32),
            pltpu.VMEM((REACH, 8, LANES), f32),
            pltpu.VMEM((RIM, chans), bf16),
            pltpu.VMEM((RIM, chans), bf16),
            pltpu.VMEM((filters // LANES, 8, LANES), f32),
            pltpu.VMEM((RIM + rows, LANES), f32),
            pltpu.VMEM((max(4, tiles // MSGS), RIM + rows, LANES), f32),
            pltpu.VMEM((tap_count, rows, LANES), f32),
            pltpu.VMEM((filters, MAXDOC), f32),
            pltpu.VMEM((tiles, REACH, LANES // fgroup * BASE, LANES), bf16),
            pltpu.VMEM((tiles, rows, LANES), f32),
            pltpu.VMEM((BASE, LANES), bf16),
            pltpu.VMEM((rows // BASE // 2, MAXDOC, LANES), bf16),
            pltpu.VMEM((rows // BASE // 2, BASE, LANES), f32),
            pltpu.VMEM((MAXDOC + rows, LANES), f32),
            pltpu.VMEM((tiles // MSGS, REACH, LANES // fgroup * PACK, LANES), f32),
            pltpu.VMEM((VIA * (tiles // MSGS), rows, LANES), bf16),
            dma((3, MSGS)),
            dma((6,)),
            dma((REACH, MSGS)),
            dma((REACH, MSGS)),
            dma((REACH,)),
            dma((REACH,)),
            dma((REACH,)),
            dma((REACH,)),
            dma,
            dma,
            dma((VIA,)),
            dma((VIA,)),
            dma((VIA,)),
        ],
        compiler_params=pltpu.CompilerParams(
            collective_id=0, has_side_effects=True, vmem_limit_bytes=48 * 1024 * 1024
        ),
    )(*(
        pltpu.with_memory_space_constraint(x, pltpu.HBM)
        for x in (gate_short, key_short, value_short, gate_long, doc_ids.reshape(1, rows), se_filter, long_filter)
    ))


def solution(mesh):
    placed = P(("groups", "ctx"), None)
    return jax.shard_map(
        body,
        mesh=mesh,
        in_specs=(placed, placed, placed, placed, P(("groups", "ctx")), P(), P()),
        out_specs=placed,
        check_vma=False,
    )
```

```python
import functools

import jax
import jax.numpy as jnp
from jax import lax
from jax.experimental import pallas as pl
from jax.experimental.pallas import tpu as pltpu
from jax.sharding import PartitionSpec as P

MAXDOC = 512
REACH = 4
RIM = 8
LANES = 128
PACK = 16
MSGS = 16
EARLY = 3
LAG1 = 2
LAG2 = 4
VIA = 2
BASE = 32
MESH = pl.DeviceIdType.MESH


def kernel(
    count, gs_hbm, k_hbm, v_hbm, gl_hbm, doc_hbm, se_hbm, h_hbm, out_ref,
    gs_ref, k_ref, v_ref, gl_ref, doc_ref, se_ref, h_ref, tail_k, tail_v,
    own, got, doc_out, got_doc, rim_out, rim_in, se_two, doc_ext, ext, agree,
    rev, taps, acc, near_mask, far_mask, out_mask, ring_all, via,
    in_sem, one_sem, send_sem, recv_sem, head_send, head_recv, doc_send, doc_recv, rim_send, rim_recv,
    via_send, via_recv, fwd_send,
):
    rows, chans = gs_ref.shape
    tap_count, filters = se_ref.shape
    fgroup = chans // filters
    per_tile = LANES // fgroup
    tiles = chans // LANES
    each = tiles // MSGS
    width = each * LANES
    half = rows // 2
    direct = MSGS - VIA
    body_rows = rows - RIM
    f32, bf16, i32 = jnp.float32, jnp.bfloat16, jnp.int32

    me = lax.axis_index("ctx")
    at = lax.rem(me, REACH)
    core = lax.rem(me, 2)
    upper = at // 2
    core_mate = me + 1 - 2 * core
    row_mate = me + 2 - 4 * upper
    has_prev = me >= REACH
    has_next = me + REACH < count
    core_filled = has_prev | (core == 1)
    row_filled = has_prev | (upper == 1)

    def local(src, dst, sem):
        return pltpu.make_async_copy(src, dst, sem)

    def piece(i, j):
        src, dst = ((k_hbm, k_ref), (v_hbm, v_ref), (gs_hbm, gs_ref))[i]
        cols = pl.ds(pl.multiple_of(j * width, width), width)
        return local(src.at[:, cols], dst.at[:, cols], in_sem.at[i, j])

    doc_in = local(doc_hbm, doc_ref, one_sem.at[0])
    tails = [
        local(k_hbm.at[pl.ds(rows - RIM, RIM), :], tail_k, one_sem.at[1]),
        local(v_hbm.at[pl.ds(rows - RIM, RIM), :], tail_v, one_sem.at[2]),
    ]
    se_in = local(se_hbm, se_ref, one_sem.at[3])
    h_in = local(h_hbm, h_ref, one_sem.at[4])
    gl_in = local(gl_hbm, gl_ref, one_sem.at[5])

    for i in range(2):
        piece(i, 0).start()
    se_in.start()
    piece(2, 0).start()
    doc_in.start()
    tails[0].start()
    tails[1].start()

    barrier = pltpu.get_barrier_semaphore()

    def greet(target):
        pl.semaphore_signal(barrier, inc=1, device_id={"ctx": target}, device_id_type=MESH)

    peers = jnp.int32(0)
    for d in range(1, REACH + 1):
        pl.when(me >= d)(lambda d=d: greet(me - d))
        pl.when(me + d < count)(lambda d=d: greet(me + d))
        peers = peers + (me >= d).astype(i32) + (me + d < count).astype(i32)

    def fetch(j, _):
        for i in range(3):
            piece(i, j).start()
        return 0

    lax.fori_loop(1, MSGS, fetch, 0)
    h_in.start()
    gl_in.start()

    lane = lax.broadcasted_iota(i32, (rows, LANES), 1)
    row = lax.broadcasted_iota(i32, (rows, LANES), 0)

    doc_in.wait()
    doc_row = jnp.broadcast_to(doc_ref[...].astype(f32), (rows, LANES))
    doc_col = doc_row.T
    doc_out[...] = doc_row[0:8]
    doc_ext[RIM:, :] = doc_col
    tails[0].wait()
    tails[1].wait()
    rim_out[...] = (tail_k[...].astype(f32) * tail_v[...].astype(f32)).astype(bf16)

    def remote(src, dst, ssem, rsem, target):
        return pltpu.make_async_remote_copy(
            src_ref=src, dst_ref=dst, send_sem=ssem, recv_sem=rsem,
            device_id={"ctx": target}, device_id_type=MESH,
        )

    def rim_copy(target):
        return remote(rim_out, rim_in, rim_send, rim_recv, target)

    def doc_copy(d, target):
        slot = REACH - d
        return remote(doc_out, got_doc.at[slot], doc_send.at[slot], doc_recv.at[slot], target)

    def msg_copy(slot, m, source, target):
        block = own if source is None else got.at[source]
        part = (pl.ds(m * each, each), pl.ds(RIM, body_rows))
        return remote(block.at[part], got.at[(slot, *part)], send_sem.at[slot], recv_sem.at[slot, m], target)

    def head_copy(slot, source, target):
        block = own if source is None else got.at[source]
        part = (pl.ds(0, tiles), pl.ds(0, RIM))
        return remote(block.at[part], got.at[(slot, *part)], head_send.at[slot], head_recv.at[slot], target)

    def send_own(copy):
        pl.when(has_next)(lambda: copy(0, None, me + REACH).start())
        pl.when(upper == 0)(lambda: copy(2, None, row_mate).start())
        pl.when(core == 0)(lambda: copy(1, None, core_mate).start())

    def msg(m):
        return lambda slot, source, target: msg_copy(slot, m, source, target)

    for tap in range(1, tap_count):
        agree[tap, RIM:, :] = (doc_ext[2 * RIM - tap : RIM + rows - tap, :] == doc_col[RIM:]).astype(f32)

    se_in.wait()
    for part in range(filters // LANES):
        se_two[part, 0:tap_count, :] = se_ref[:, part * LANES : (part + 1) * LANES]
        se_two[part, tap_count:, :] = jnp.zeros((8 - tap_count, LANES), f32)

    tiles_per_part = LANES // per_tile
    spread = lax.broadcasted_iota(i32, (8, LANES), 1) // fgroup

    def weights_of(ct):
        index = spread + lax.rem(ct, tiles_per_part) * per_tile
        return jnp.take_along_axis(se_two[ct // tiles_per_part], index, axis=1)

    def lanes_of(ct):
        return pl.ds(pl.multiple_of(ct * LANES, LANES), LANES)

    def product(ct, part):
        lanes = lanes_of(ct)
        return (k_ref[part, lanes].astype(f32) * v_ref[part, lanes].astype(f32)).astype(bf16).astype(f32)

    def await_piece(j, _):
        for i in range(3):
            piece(i, j).wait()
        return 0

    def short_body(j, _):
        for u in range(each):
            ct = j * each + u
            weights = weights_of(ct)
            kv = product(ct, slice(None))
            ext[u, RIM:, :] = kv
            total = kv[RIM:] * weights[0:1, :]
            for tap in range(1, tap_count):
                shifted = ext[u, 2 * RIM - tap : RIM + rows - tap, :]
                total = total + (shifted * agree[tap, RIM:, :]) * weights[tap : tap + 1, :]
            mixed = gs_ref[RIM:, lanes_of(ct)].astype(f32) * total
            own[ct, RIM:, :] = mixed.astype(bf16)
        return 0

    def early_body(j, _):
        await_piece(j, 0)
        return short_body(j, 0)

    lax.fori_loop(0, EARLY, early_body, 0)
    lax.fori_loop(direct, MSGS, early_body, 0)

    pl.semaphore_wait(barrier, peers)
    pl.when(me + 1 < count)(lambda: rim_copy(me + 1).start())
    for d in range(1, REACH + 1):
        pl.when(me + d < count)(lambda d=d: doc_copy(d, me + d).start())

    def send_msg(j, _):
        send_own(msg(j))
        return 0

    def side(i):
        return pl.ds(i * each, each), pl.ds(RIM, body_rows)

    def via_copy(i, target):
        block = own.at[pl.ds((direct + i) * each, each), pl.ds(RIM, body_rows)]
        return remote(block, via.at[side(i)], via_send.at[i], via_recv.at[i], target)

    def fwd_copy(i, target):
        m = direct + i
        block = got.at[2, pl.ds(m * each, each), pl.ds(RIM, body_rows)]
        return remote(via.at[side(i)], block, fwd_send.at[i], recv_sem.at[2, m], target)

    for i in range(VIA):
        pl.when((upper == 1) & has_next)(lambda i=i: via_copy(i, row_mate).start())
    lax.fori_loop(0, EARLY, send_msg, 0)


    def clear(slot):
        got[slot] = jnp.zeros(got.shape[1:], bf16)

    @pl.when(jnp.logical_not(has_prev))
    def _():
        clear(0)
        pl.when(core == 0)(lambda: clear(1))
        pl.when(upper == 0)(lambda: clear(2))
        pl.when(upper == 0)(lambda: clear(3))

    h_in.wait()
    lag = lax.broadcasted_iota(i32, (LANES, LANES), 0)
    pos = lax.broadcasted_iota(i32, (LANES, LANES), 1)
    flip = jnp.where(lag == lax.rem(LANES - pos, LANES), 1.0, 0.0).astype(bf16)
    for d in range(REACH):
        cols = slice(d * LANES, (d + 1) * LANES)
        rev[:, cols] = jnp.dot(h_ref[:, cols], flip, preferred_element_type=f32)

    low = lane[:half] < half
    causal = lane[:half] <= row[:half]
    same_low = doc_col[:half] == doc_row[:half]
    same_high = doc_col[half:] == pltpu.roll(doc_row[:half], half, 1)
    late = same_high.astype(f32)
    early = causal.astype(f32) * same_low.astype(f32)
    near_mask[0] = jnp.where(low, early, late).astype(bf16)
    near_mask[1] = jnp.where(low, causal.astype(f32) * late, 0.0).astype(bf16)
    leader = jnp.broadcast_to(doc_row[0:1, 0:1], (rows, LANES))
    out_mask[...] = (doc_col == leader).astype(f32)

    for w in range(REACH):
        pl.when(me >= REACH - w)(lambda w=w: doc_copy(REACH - w, core_mate).wait_recv())

        @pl.when(me < REACH - w)
        def _():
            got_doc[w] = jnp.full((8, LANES), -1.0, f32)

        source_col = jnp.broadcast_to(got_doc[w, 0:1, :], (rows, LANES)).T
        far_mask[w] = (source_col == leader).astype(bf16)
        if w == REACH - 1:
            doc_ext[0:RIM, :] = source_col[rows - RIM :]

    @pl.when(me == 0)
    def _():
        rim_in[...] = jnp.zeros((RIM, chans), bf16)

    @pl.when(me > 0)
    def _():
        rim_copy(core_mate).wait_recv()

    for tap in range(1, tap_count):
        agree[tap, 0:RIM, :] = (doc_ext[RIM - tap : 2 * RIM - tap, :] == doc_col[0:RIM]).astype(f32)

    lax.fori_loop(EARLY, direct, await_piece, 0)

    def short_head(j, _):
        for u in range(4):
            ct = j * 4 + u
            weights = weights_of(ct)
            kv = product(ct, slice(0, RIM))
            ext[u, 0:RIM, :] = rim_in[:, lanes_of(ct)].astype(f32)
            ext[u, RIM : 2 * RIM, :] = kv
            total = kv * weights[0:1, :]
            for tap in range(1, tap_count):
                shifted = ext[u, RIM - tap : 2 * RIM - tap, :]
                total = total + (shifted * agree[tap, 0:RIM, :]) * weights[tap : tap + 1, :]
            mixed = gs_ref[0:RIM, lanes_of(ct)].astype(f32) * total
            own[ct, 0:RIM, :] = mixed.astype(bf16)
        return 0

    lax.fori_loop(0, tiles // 4, short_head, 0)
    send_own(head_copy)

    @pl.when((upper == 0) & has_next)
    def _():
        for i in range(VIA):
            via_copy(i, row_mate).wait_recv()
            fwd_copy(i, me + REACH).start()

    gl_in.wait()

    tile_group = lax.broadcasted_iota(i32, (1, LANES), 1) // fgroup
    half_group = lax.rem(tile_group, per_tile // 2)
    low_half = lax.broadcasted_iota(i32, (1, LANES), 1) < half

    def pick(result, group, groups, height, lanes):
        picked = result[0:height, lanes]
        for g in range(1, groups):
            picked = jnp.where(group == g, result[g * height : (g + 1) * height, lanes], picked)
        return picked

    below = [lane[0:PACK] <= row[0:PACK] + r * PACK for r in range(BASE // PACK)]

    def prepare(ct, ring_rows):
        first = pl.multiple_of(ct * per_tile, per_tile)
        filt = rev[pl.ds(first, per_tile), :]
        for d in range(REACH):
            line = filt[:, d * LANES : (d + 1) * LANES]
            for i in range(PACK):
                ring_rows[d, pl.ds(i, per_tile, stride=PACK), :] = line if i == 0 else pltpu.roll(line, i, 1)
        zero = jnp.zeros((PACK, LANES), bf16)
        near = []
        for g in range(per_tile):
            ring = [ring_rows[d, g * PACK : (g + 1) * PACK, :].astype(bf16) for d in range(REACH)]
            for r in range(BASE // PACK):
                turned = ring if r == 0 else [pltpu.roll(c, r * PACK, 1) for c in ring]
                at_row = g * BASE + r * PACK
                for w in range(REACH):
                    d = REACH - w
                    recent = turned[d] if d < REACH else zero
                    taps[ct, w, at_row : at_row + PACK, :] = jnp.where(below[r], recent, turned[d - 1])
            for r in range(half // PACK):
                turned = ring[0] if r == 0 else pltpu.roll(ring[0], r * PACK, 1)
                at_mask = slice(r * PACK, (r + 1) * PACK)
                near.append(jnp.concatenate([turned * near_mask[0, at_mask], turned * near_mask[1, at_mask]], 1))
        block = own[ct]
        first_half, second_half = block[:half], block[half:]
        none = jnp.zeros((half, LANES), bf16)
        right = jnp.concatenate(
            [
                jnp.concatenate([first_half, none, none, none], 0),
                jnp.concatenate([none, first_half, second_half, none], 0),
            ],
            1,
        )
        result = jnp.dot(jnp.concatenate(near, 0), right, preferred_element_type=f32)
        acc[ct, 0:half, :] = pick(result, tile_group, per_tile, half, slice(0, LANES))
        acc[ct, half:, :] = pick(result, tile_group, per_tile, half, slice(LANES, 2 * LANES))

    slots = []
    for w in range(REACH):
        q = lax.rem(at + w, REACH)
        slots.append(lax.rem(q // 2 + upper, 2) * 2 + lax.rem(q + at, 2))

    def far(ct):
        left = jnp.concatenate([got[slots[w], ct] * far_mask[w] for w in range(REACH)], 0)
        gap = jnp.zeros((BASE, LANES), bf16)
        later = jnp.concatenate([left[BASE:], gap], 0)
        outs = []
        for h in range(2):
            if h == 0:
                pair = jnp.where(low_half, left, pltpu.roll(later, half, 1))
            else:
                pair = jnp.where(low_half, pltpu.roll(left, half, 1), later)
            wide = jnp.concatenate([pair, jnp.concatenate([pair[2 * BASE :], gap, gap], 0)], 1)
            height = per_tile // 2 * BASE
            lhs = jnp.concatenate([taps[ct, w, h * height : (h + 1) * height, :] for w in range(REACH)], 1)
            result = jnp.dot(lhs, wide, preferred_element_type=f32)
            outs.append(
                [pick(result, half_group, per_tile // 2, BASE, slice(p * LANES, (p + 1) * LANES)) for p in range(2)]
            )
        both = []
        for p in range(2):
            both.append(jnp.where(low_half, outs[0][p], pltpu.roll(outs[1][p], half, 1)))
            both.append(jnp.where(low_half, pltpu.roll(outs[0][p], half, 1), outs[1][p]))
        total = acc[ct] + jnp.concatenate(both, 0) * out_mask[...]
        out_ref[:, lanes_of(ct)] = (gl_ref[:, lanes_of(ct)].astype(f32) * total).astype(bf16)

    def step(s, _):
        @pl.when(s < MSGS - EARLY)
        def _():
            @pl.when(s < direct - EARLY)
            def _():
                short_body(s + EARLY, 0)

            send_own(msg(s + EARLY))

        def prepared(s):
            return jnp.minimum(jnp.minimum(s, (s + EARLY) // 2), MSGS // 2)

        @pl.when(prepared(s + 1) > prepared(s))
        def _():
            for u in range(2 * each):
                prepare(prepared(s) * (2 * each) + u, ring_all.at[u])

        @pl.when(s < MSGS)
        def _():
            def relay(copy, row_too=True):
                pl.when(has_prev)(lambda: copy(0, None, core_mate).wait_recv())
                pl.when(has_prev & (upper == 1) & row_too)(lambda: copy(2, 0, row_mate).start())
                pl.when(has_prev & (core == 1))(lambda: copy(1, 0, core_mate).start())

            pl.when(s == EARLY)(lambda: relay(head_copy))
            relay(msg(s), s < direct)

        @pl.when((s >= LAG1) & (s < MSGS + LAG1))
        def _():
            def relay(copy):
                pl.when(row_filled)(lambda: copy(2, None, core_mate).wait_recv())
                pl.when(row_filled)(lambda: copy(3, 2, core_mate).start())

            pl.when(s == EARLY + LAG1)(lambda: relay(head_copy))
            relay(msg(s - LAG1))

        def finished(s):
            paired = (s - LAG2) // 2 * 2
            done = jnp.where(s <= MSGS, paired, s - LAG2)
            return jnp.where(s <= EARLY + LAG1 + 1, 0, done)

        def far_msgs(m, many):
            def arrive(copy):
                pl.when(core_filled)(lambda: copy(1, None, core_mate).wait_recv())
                pl.when(row_filled)(lambda: copy(3, None, core_mate).wait_recv())

            pl.when(m == 0)(lambda: arrive(head_copy))
            for i in range(many):
                arrive(msg(m + i))
            for u in range(many * each):
                far(m * each + u)

        for many in (1, 2):
            pl.when(finished(s + 1) - finished(s) == many)(lambda many=many: far_msgs(finished(s), many))

        return 0

    lax.fori_loop(0, MSGS + LAG2, step, 0)

    def drain(slot, msgs):
        part = (pl.ds(0, msgs * each), pl.ds(RIM, body_rows))
        block = own.at[part]
        remote(block, got.at[(slot, *part)], send_sem.at[slot], recv_sem.at[slot, 0], core_mate).wait_send()
        head_copy(slot, None, core_mate).wait_send()

    pl.when(has_next)(lambda: drain(0, MSGS))
    pl.when(has_prev | (core == 0))(lambda: drain(1, MSGS))
    pl.when(upper == 0)(lambda: drain(2, MSGS))
    pl.when(has_prev & (upper == 1))(lambda: drain(2, direct))
    pl.when(row_filled)(lambda: drain(3, MSGS))
    for i in range(VIA):
        pl.when((upper == 1) & has_next)(lambda i=i: via_copy(i, core_mate).wait_send())
        pl.when((upper == 0) & has_next)(lambda i=i: fwd_copy(i, core_mate).wait_send())
    pl.when(me + 1 < count)(lambda: rim_copy(core_mate).wait_send())
    for d in range(1, REACH + 1):
        pl.when(me + d < count)(lambda d=d: doc_copy(d, core_mate).wait_send())


def body(gate_short, key_short, value_short, gate_long, doc_ids, se_filter, long_filter):
    rows, chans = gate_short.shape
    tap_count, filters = se_filter.shape
    fgroup = chans // filters
    count = lax.axis_size("ctx")
    tiles = chans // LANES
    assert rows * REACH == MAXDOC and rows == LANES and count % REACH == 0
    assert tap_count <= RIM and LANES % fgroup == 0 and filters % LANES == 0
    assert tiles % MSGS == 0 and tiles % 4 == 0 and long_filter.shape[1] == MAXDOC
    bf16, f32 = jnp.bfloat16, jnp.float32
    anywhere = pl.BlockSpec(memory_space=pl.ANY)
    dma = pltpu.SemaphoreType.DMA
    return pl.pallas_call(
        functools.partial(kernel, count),
        out_shape=pltpu.VMEM((rows, chans), bf16),
        in_specs=[anywhere] * 7,
        out_specs=pl.BlockSpec(memory_space=pltpu.VMEM),
        scratch_shapes=[
            pltpu.VMEM((rows, chans), bf16),
            pltpu.VMEM((rows, chans), bf16),
            pltpu.VMEM((rows, chans), bf16),
            pltpu.VMEM((rows, chans), bf16),
            pltpu.VMEM((1, rows), jnp.int32),
            pltpu.VMEM((tap_count, filters), f32),
            pltpu.VMEM((filters, MAXDOC), bf16),
            pltpu.VMEM((RIM, chans), bf16),
            pltpu.VMEM((RIM, chans), bf16),
            pltpu.VMEM((tiles, rows, LANES), bf16),
            pltpu.VMEM((REACH, tiles, rows, LANES), bf16),
            pltpu.VMEM((8, LANES), f32),
            pltpu.VMEM((REACH, 8, LANES), f32),
            pltpu.VMEM((RIM, chans), bf16),
            pltpu.VMEM((RIM, chans), bf16),
            pltpu.VMEM((filters // LANES, 8, LANES), f32),
            pltpu.VMEM((RIM + rows, LANES), f32),
            pltpu.VMEM((max(4, tiles // MSGS), RIM + rows, LANES), f32),
            pltpu.VMEM((tap_count, rows, LANES), f32),
            pltpu.VMEM((filters, MAXDOC), f32),
            pltpu.VMEM((tiles, REACH, LANES // fgroup * BASE, LANES), bf16),
            pltpu.VMEM((tiles, rows, LANES), f32),
            pltpu.VMEM((2, rows // 2, LANES), bf16),
            pltpu.VMEM((REACH, rows, LANES), bf16),
            pltpu.VMEM((rows, LANES), f32),
            pltpu.VMEM((2 * (tiles // MSGS), REACH, LANES // fgroup * PACK, LANES), f32),
            pltpu.VMEM((VIA * (tiles // MSGS), rows, LANES), bf16),
            dma((3, MSGS)),
            dma((6,)),
            dma((REACH,)),
            dma((REACH, MSGS)),
            dma((REACH,)),
            dma((REACH,)),
            dma((REACH,)),
            dma((REACH,)),
            dma,
            dma,
            dma((VIA,)),
            dma((VIA,)),
            dma((VIA,)),
        ],
        compiler_params=pltpu.CompilerParams(
            collective_id=0, has_side_effects=True, vmem_limit_bytes=48 * 1024 * 1024
        ),
    )(*(
        pltpu.with_memory_space_constraint(x, pltpu.HBM)
        for x in (gate_short, key_short, value_short, gate_long, doc_ids.reshape(1, rows), se_filter, long_filter)
    ))


def solution(mesh):
    placed = P(("groups", "ctx"), None)
    return jax.shard_map(
        body,
        mesh=mesh,
        in_specs=(placed, placed, placed, placed, P(("groups", "ctx")), P(), P()),
        out_specs=placed,
        check_vma=False,
    )
```

```python
import functools

import jax
import jax.numpy as jnp
from jax import lax
from jax.experimental import pallas as pl
from jax.experimental.pallas import tpu as pltpu
from jax.sharding import PartitionSpec as P

MAXDOC = 512
REACH = 4
RIM = 8
LANES = 128
PACK = 16
MSGS = 16
EARLY = 3
LAG1 = 2
LAG2 = 4
VIA = 2
GROUPS = 4
FIRST = 2
AHEAD = 2
BASE = 32
MESH = pl.DeviceIdType.MESH


def kernel(
    count, gs_hbm, k_hbm, v_hbm, gl_hbm, doc_hbm, se_hbm, h_hbm, out_ref,
    gs_ref, k_ref, v_ref, gl_ref, doc_ref, se_ref, h_ref, tail_k, tail_v,
    own, got, doc_out, got_doc, rim_out, rim_in, se_two, doc_ext, ext, agree,
    rev, taps, acc, near_mask, far_mask, out_mask, ring_all, close, via,
    in_sem, one_sem, send_sem, recv_sem, head_send, head_recv, doc_send, doc_recv, rim_send, rim_recv,
    via_send, via_recv, fwd_send,
):
    rows, chans = gs_ref.shape
    tap_count, filters = se_ref.shape
    fgroup = chans // filters
    per_tile = LANES // fgroup
    tiles = chans // LANES
    each = tiles // MSGS
    width = each * LANES
    half = rows // 2
    direct = MSGS - VIA
    body_rows = rows - RIM
    f32, bf16, i32 = jnp.float32, jnp.bfloat16, jnp.int32

    me = lax.axis_index("ctx")
    at = lax.rem(me, REACH)
    core = lax.rem(me, 2)
    upper = at // 2
    core_mate = me + 1 - 2 * core
    row_mate = me + 2 - 4 * upper
    has_prev = me >= REACH
    has_next = me + REACH < count
    core_filled = has_prev | (core == 1)
    row_filled = has_prev | (upper == 1)

    def local(src, dst, sem):
        return pltpu.make_async_copy(src, dst, sem)

    def piece(i, j):
        src, dst = ((k_hbm, k_ref), (v_hbm, v_ref), (gs_hbm, gs_ref))[i]
        cols = slice(j * chans // GROUPS, (j + 1) * chans // GROUPS)
        return local(src.at[:, cols], dst.at[:, cols], in_sem.at[i, j])

    doc_in = local(doc_hbm, doc_ref, one_sem.at[0])
    tails = [
        local(k_hbm.at[pl.ds(rows - RIM, RIM), :], tail_k, one_sem.at[1]),
        local(v_hbm.at[pl.ds(rows - RIM, RIM), :], tail_v, one_sem.at[2]),
    ]
    se_in = local(se_hbm, se_ref, one_sem.at[3])
    h_in = local(h_hbm, h_ref, one_sem.at[4])
    gl_in = local(gl_hbm, gl_ref, one_sem.at[5])

    for i in range(2):
        piece(i, 0).start()
    se_in.start()
    piece(2, 0).start()
    doc_in.start()
    tails[0].start()
    tails[1].start()

    barrier = pltpu.get_barrier_semaphore()

    def greet(target):
        pl.semaphore_signal(barrier, inc=1, device_id={"ctx": target}, device_id_type=MESH)

    peers = jnp.int32(0)
    for d in range(1, REACH + 1):
        pl.when(me >= d)(lambda d=d: greet(me - d))
        pl.when(me + d < count)(lambda d=d: greet(me + d))
        peers = peers + (me >= d).astype(i32) + (me + d < count).astype(i32)

    for j in (GROUPS - 1, *range(1, GROUPS - 1)):
        for i in range(3):
            piece(i, j).start()
    h_in.start()
    gl_in.start()

    lane = lax.broadcasted_iota(i32, (rows, LANES), 1)
    row = lax.broadcasted_iota(i32, (rows, LANES), 0)

    doc_in.wait()
    doc_row = jnp.broadcast_to(doc_ref[...].astype(f32), (rows, LANES))
    doc_col = doc_row.T
    doc_out[...] = doc_row[0:8]
    doc_ext[RIM:, :] = doc_col
    tails[0].wait()
    tails[1].wait()
    rim_out[...] = (tail_k[...].astype(f32) * tail_v[...].astype(f32)).astype(bf16)

    def remote(src, dst, ssem, rsem, target):
        return pltpu.make_async_remote_copy(
            src_ref=src, dst_ref=dst, send_sem=ssem, recv_sem=rsem,
            device_id={"ctx": target}, device_id_type=MESH,
        )

    def rim_copy(target):
        return remote(rim_out, rim_in, rim_send, rim_recv, target)

    def doc_copy(d, target):
        slot = REACH - d
        return remote(doc_out, got_doc.at[slot], doc_send.at[slot], doc_recv.at[slot], target)

    def msg_copy(slot, m, source, target):
        block = own if source is None else got.at[source]
        part = (pl.ds(m * each, each), pl.ds(RIM, body_rows))
        return remote(block.at[part], got.at[(slot, *part)], send_sem.at[slot], recv_sem.at[slot, m], target)

    def head_copy(slot, source, target):
        block = own if source is None else got.at[source]
        part = (pl.ds(0, tiles), pl.ds(0, RIM))
        return remote(block.at[part], got.at[(slot, *part)], head_send.at[slot], head_recv.at[slot], target)

    def send_own(copy):
        pl.when(has_next)(lambda: copy(0, None, me + REACH).start())
        pl.when(upper == 0)(lambda: copy(2, None, row_mate).start())
        pl.when(core == 0)(lambda: copy(1, None, core_mate).start())

    def msg(m):
        return lambda slot, source, target: msg_copy(slot, m, source, target)

    for tap in range(1, tap_count):
        agree[tap, RIM:, :] = (doc_ext[2 * RIM - tap : RIM + rows - tap, :] == doc_col[RIM:]).astype(f32)

    se_in.wait()
    for part in range(filters // LANES):
        se_two[part, 0:tap_count, :] = se_ref[:, part * LANES : (part + 1) * LANES]
        se_two[part, tap_count:, :] = jnp.zeros((8 - tap_count, LANES), f32)

    tiles_per_part = LANES // per_tile
    spread = lax.broadcasted_iota(i32, (8, LANES), 1) // fgroup

    def weights_of(ct):
        index = spread + lax.rem(ct, tiles_per_part) * per_tile
        return jnp.take_along_axis(se_two[ct // tiles_per_part], index, axis=1)

    def lanes_of(ct):
        return pl.ds(pl.multiple_of(ct * LANES, LANES), LANES)

    def product(ct, part):
        lanes = lanes_of(ct)
        return (k_ref[part, lanes].astype(f32) * v_ref[part, lanes].astype(f32)).astype(bf16).astype(f32)

    def await_pieces(j):
        for i in range(3):
            piece(i, j).wait()

    def short_body(j, _):
        for u in range(each):
            ct = j * each + u
            weights = weights_of(ct)
            kv = product(ct, slice(None))
            ext[u, RIM:, :] = kv
            total = kv[RIM:] * weights[0:1, :]
            for tap in range(1, tap_count):
                shifted = ext[u, 2 * RIM - tap : RIM + rows - tap, :]
                total = total + (shifted * agree[tap, RIM:, :]) * weights[tap : tap + 1, :]
            mixed = gs_ref[RIM:, lanes_of(ct)].astype(f32) * total
            own[ct, RIM:, :] = mixed.astype(bf16)
        return 0

    await_pieces(0)
    lax.fori_loop(0, FIRST, short_body, 0)

    pl.semaphore_wait(barrier, peers)
    pl.when(me + 1 < count)(lambda: rim_copy(me + 1).start())
    for d in range(1, REACH + 1):
        pl.when(me + d < count)(lambda d=d: doc_copy(d, me + d).start())

    def send_msg(j, _):
        send_own(msg(j))
        return 0

    def side(i):
        return pl.ds(i * each, each), pl.ds(RIM, body_rows)

    def via_copy(i, target):
        block = own.at[pl.ds((direct + i) * each, each), pl.ds(RIM, body_rows)]
        return remote(block, via.at[side(i)], via_send.at[i], via_recv.at[i], target)

    def fwd_copy(i, target):
        m = direct + i
        block = got.at[2, pl.ds(m * each, each), pl.ds(RIM, body_rows)]
        return remote(via.at[side(i)], block, fwd_send.at[i], recv_sem.at[2, m], target)

    lax.fori_loop(0, FIRST, send_msg, 0)
    await_pieces(GROUPS - 1)
    lax.fori_loop(direct, MSGS, short_body, 0)
    for i in range(VIA):
        pl.when((upper == 1) & has_next)(lambda i=i: via_copy(i, row_mate).start())
    lax.fori_loop(FIRST, EARLY, lambda j, c: send_msg(j, short_body(j, c)), 0)


    def clear(slot):
        got[slot] = jnp.zeros(got.shape[1:], bf16)

    @pl.when(jnp.logical_not(has_prev))
    def _():
        clear(0)
        pl.when(core == 0)(lambda: clear(1))
        pl.when(upper == 0)(lambda: clear(2))
        pl.when(upper == 0)(lambda: clear(3))

    h_in.wait()
    lag = lax.broadcasted_iota(i32, (LANES, LANES), 0)
    pos = lax.broadcasted_iota(i32, (LANES, LANES), 1)
    flip = jnp.where(lag == lax.rem(LANES - pos, LANES), 1.0, 0.0).astype(bf16)
    for d in range(REACH):
        cols = slice(d * LANES, (d + 1) * LANES)
        rev[:, cols] = jnp.dot(h_ref[:, cols], flip, preferred_element_type=f32)

    low = lane[:half] < half
    causal = lane[:half] <= row[:half]
    same_low = doc_col[:half] == doc_row[:half]
    same_high = doc_col[half:] == pltpu.roll(doc_row[:half], half, 1)
    late = same_high.astype(f32)
    early = causal.astype(f32) * same_low.astype(f32)
    near_mask[0] = jnp.where(low, early, late).astype(bf16)
    near_mask[1] = jnp.where(low, causal.astype(f32) * late, 0.0).astype(bf16)
    leader = jnp.broadcast_to(doc_row[0:1, 0:1], (rows, LANES))
    out_mask[...] = (doc_col == leader).astype(f32)

    below = [lane[0:PACK] <= row[0:PACK] + r * PACK for r in range(BASE // PACK)]

    def build_taps(ct, ring_rows):
        first = pl.multiple_of(ct * per_tile, per_tile)
        filt = rev[pl.ds(first, per_tile), :]
        for d in range(REACH):
            line = filt[:, d * LANES : (d + 1) * LANES]
            for i in range(PACK):
                ring_rows[d, pl.ds(i, per_tile, stride=PACK), :] = line if i == 0 else pltpu.roll(line, i, 1)
        zero = jnp.zeros((PACK, LANES), bf16)
        for g in range(per_tile):
            ring = [ring_rows[d, g * PACK : (g + 1) * PACK, :].astype(bf16) for d in range(REACH)]
            for r in range(BASE // PACK):
                turned = ring if r == 0 else [pltpu.roll(c, r * PACK, 1) for c in ring]
                at_row = g * BASE + r * PACK
                for w in range(REACH):
                    d = REACH - w
                    recent = turned[d] if d < REACH else zero
                    taps[ct, w, at_row : at_row + PACK, :] = jnp.where(below[r], recent, turned[d - 1])
        return ring_rows[0].astype(bf16)

    def build_ahead(q, _):
        for u in range(2 * each):
            ct = q * (2 * each) + u
            close[ct] = build_taps(ct, ring_all.at[u])
        return 0

    lax.fori_loop(0, AHEAD, build_ahead, 0)

    for w in range(REACH):
        pl.when(me >= REACH - w)(lambda w=w: doc_copy(REACH - w, core_mate).wait_recv())

        @pl.when(me < REACH - w)
        def _():
            got_doc[w] = jnp.full((8, LANES), -1.0, f32)

        source_col = jnp.broadcast_to(got_doc[w, 0:1, :], (rows, LANES)).T
        far_mask[w] = (source_col == leader).astype(bf16)
        if w == REACH - 1:
            doc_ext[0:RIM, :] = source_col[rows - RIM :]

    @pl.when(me == 0)
    def _():
        rim_in[...] = jnp.zeros((RIM, chans), bf16)

    @pl.when(me > 0)
    def _():
        rim_copy(core_mate).wait_recv()

    for tap in range(1, tap_count):
        agree[tap, 0:RIM, :] = (doc_ext[RIM - tap : 2 * RIM - tap, :] == doc_col[0:RIM]).astype(f32)

    for j in range(1, GROUPS - 1):
        await_pieces(j)

    def short_head(j, _):
        for u in range(4):
            ct = j * 4 + u
            weights = weights_of(ct)
            kv = product(ct, slice(0, RIM))
            ext[u, 0:RIM, :] = rim_in[:, lanes_of(ct)].astype(f32)
            ext[u, RIM : 2 * RIM, :] = kv
            total = kv * weights[0:1, :]
            for tap in range(1, tap_count):
                shifted = ext[u, RIM - tap : 2 * RIM - tap, :]
                total = total + (shifted * agree[tap, 0:RIM, :]) * weights[tap : tap + 1, :]
            mixed = gs_ref[0:RIM, lanes_of(ct)].astype(f32) * total
            own[ct, 0:RIM, :] = mixed.astype(bf16)
        return 0

    lax.fori_loop(0, tiles // 4, short_head, 0)
    send_own(head_copy)

    @pl.when((upper == 0) & has_next)
    def _():
        for i in range(VIA):
            via_copy(i, row_mate).wait_recv()
            fwd_copy(i, me + REACH).start()

    gl_in.wait()

    tile_group = lax.broadcasted_iota(i32, (1, LANES), 1) // fgroup
    half_group = lax.rem(tile_group, per_tile // 2)
    low_half = lax.broadcasted_iota(i32, (1, LANES), 1) < half

    def pick(result, group, groups, height, lanes):
        picked = result[0:height, lanes]
        for g in range(1, groups):
            picked = jnp.where(group == g, result[g * height : (g + 1) * height, lanes], picked)
        return picked

    def near_part(ct, close_rows):
        near = []
        for g in range(per_tile):
            ring = close_rows[g * PACK : (g + 1) * PACK]
            for r in range(half // PACK):
                turned = ring if r == 0 else pltpu.roll(ring, r * PACK, 1)
                at_mask = slice(r * PACK, (r + 1) * PACK)
                near.append(jnp.concatenate([turned * near_mask[0, at_mask], turned * near_mask[1, at_mask]], 1))
        block = own[ct]
        first_half, second_half = block[:half], block[half:]
        none = jnp.zeros((half, LANES), bf16)
        right = jnp.concatenate(
            [
                jnp.concatenate([first_half, none, none, none], 0),
                jnp.concatenate([none, first_half, second_half, none], 0),
            ],
            1,
        )
        result = jnp.dot(jnp.concatenate(near, 0), right, preferred_element_type=f32)
        acc[ct, 0:half, :] = pick(result, tile_group, per_tile, half, slice(0, LANES))
        acc[ct, half:, :] = pick(result, tile_group, per_tile, half, slice(LANES, 2 * LANES))

    slots = []
    for w in range(REACH):
        q = lax.rem(at + w, REACH)
        slots.append(lax.rem(q // 2 + upper, 2) * 2 + lax.rem(q + at, 2))

    def far(ct):
        left = jnp.concatenate([got[slots[w], ct] * far_mask[w] for w in range(REACH)], 0)
        gap = jnp.zeros((BASE, LANES), bf16)
        later = jnp.concatenate([left[BASE:], gap], 0)
        outs = []
        for h in range(2):
            if h == 0:
                pair = jnp.where(low_half, left, pltpu.roll(later, half, 1))
            else:
                pair = jnp.where(low_half, pltpu.roll(left, half, 1), later)
            wide = jnp.concatenate([pair, jnp.concatenate([pair[2 * BASE :], gap, gap], 0)], 1)
            height = per_tile // 2 * BASE
            lhs = jnp.concatenate([taps[ct, w, h * height : (h + 1) * height, :] for w in range(REACH)], 1)
            result = jnp.dot(lhs, wide, preferred_element_type=f32)
            outs.append(
                [pick(result, half_group, per_tile // 2, BASE, slice(p * LANES, (p + 1) * LANES)) for p in range(2)]
            )
        both = []
        for p in range(2):
            both.append(jnp.where(low_half, outs[0][p], pltpu.roll(outs[1][p], half, 1)))
            both.append(jnp.where(low_half, pltpu.roll(outs[0][p], half, 1), outs[1][p]))
        total = acc[ct] + jnp.concatenate(both, 0) * out_mask[...]
        out_ref[:, lanes_of(ct)] = (gl_ref[:, lanes_of(ct)].astype(f32) * total).astype(bf16)

    def step(s, _):
        @pl.when(s < MSGS - EARLY)
        def _():
            @pl.when(s < direct - EARLY)
            def _():
                short_body(s + EARLY, 0)

            send_own(msg(s + EARLY))

        def prepared(s):
            return jnp.minimum(jnp.minimum(s, (s + EARLY) // 2), MSGS // 2)

        group = prepared(s)
        fresh = prepared(s + 1) > group

        @pl.when(fresh & (group < AHEAD))
        def _():
            for u in range(2 * each):
                ct = group * (2 * each) + u
                near_part(ct, close[ct])

        @pl.when(fresh & (group >= AHEAD))
        def _():
            for u in range(2 * each):
                ct = group * (2 * each) + u
                near_part(ct, build_taps(ct, ring_all.at[u]))

        @pl.when(s < MSGS)
        def _():
            def relay(copy, row_too=True):
                pl.when(has_prev)(lambda: copy(0, None, core_mate).wait_recv())
                pl.when(has_prev & (upper == 1) & row_too)(lambda: copy(2, 0, row_mate).start())
                pl.when(has_prev & (core == 1))(lambda: copy(1, 0, core_mate).start())

            pl.when(s == EARLY)(lambda: relay(head_copy))
            relay(msg(s), s < direct)

        @pl.when((s >= LAG1) & (s < MSGS + LAG1))
        def _():
            def relay(copy):
                pl.when(row_filled)(lambda: copy(2, None, core_mate).wait_recv())
                pl.when(row_filled)(lambda: copy(3, 2, core_mate).start())

            pl.when(s == EARLY + LAG1)(lambda: relay(head_copy))
            relay(msg(s - LAG1))

        def finished(s):
            paired = (s - LAG2) // 2 * 2
            done = jnp.where(s <= MSGS, paired, s - LAG2)
            return jnp.where(s <= EARLY + LAG1 + 1, 0, done)

        def far_msgs(m, many):
            def arrive(copy):
                pl.when(core_filled)(lambda: copy(1, None, core_mate).wait_recv())
                pl.when(row_filled)(lambda: copy(3, None, core_mate).wait_recv())

            pl.when(m == 0)(lambda: arrive(head_copy))
            for i in range(many):
                arrive(msg(m + i))
            for u in range(many * each):
                far(m * each + u)

        for many in (1, 2):
            pl.when(finished(s + 1) - finished(s) == many)(lambda many=many: far_msgs(finished(s), many))

        return 0

    lax.fori_loop(0, MSGS + LAG2, step, 0)

    def drain(slot, msgs):
        part = (pl.ds(0, msgs * each), pl.ds(RIM, body_rows))
        block = own.at[part]
        remote(block, got.at[(slot, *part)], send_sem.at[slot], recv_sem.at[slot, 0], core_mate).wait_send()
        head_copy(slot, None, core_mate).wait_send()

    pl.when(has_next)(lambda: drain(0, MSGS))
    pl.when(has_prev | (core == 0))(lambda: drain(1, MSGS))
    pl.when(upper == 0)(lambda: drain(2, MSGS))
    pl.when(has_prev & (upper == 1))(lambda: drain(2, direct))
    pl.when(row_filled)(lambda: drain(3, MSGS))
    for i in range(VIA):
        pl.when((upper == 1) & has_next)(lambda i=i: via_copy(i, core_mate).wait_send())
        pl.when((upper == 0) & has_next)(lambda i=i: fwd_copy(i, core_mate).wait_send())
    pl.when(me + 1 < count)(lambda: rim_copy(core_mate).wait_send())
    for d in range(1, REACH + 1):
        pl.when(me + d < count)(lambda d=d: doc_copy(d, core_mate).wait_send())


def body(gate_short, key_short, value_short, gate_long, doc_ids, se_filter, long_filter):
    rows, chans = gate_short.shape
    tap_count, filters = se_filter.shape
    fgroup = chans // filters
    count = lax.axis_size("ctx")
    tiles = chans // LANES
    assert rows * REACH == MAXDOC and rows == LANES and count % REACH == 0
    assert tap_count <= RIM and LANES % fgroup == 0 and filters % LANES == 0
    assert tiles % MSGS == 0 and tiles % 4 == 0 and long_filter.shape[1] == MAXDOC
    bf16, f32 = jnp.bfloat16, jnp.float32
    anywhere = pl.BlockSpec(memory_space=pl.ANY)
    dma = pltpu.SemaphoreType.DMA
    return pl.pallas_call(
        functools.partial(kernel, count),
        out_shape=pltpu.VMEM((rows, chans), bf16),
        in_specs=[anywhere] * 7,
        out_specs=pl.BlockSpec(memory_space=pltpu.VMEM),
        scratch_shapes=[
            pltpu.VMEM((rows, chans), bf16),
            pltpu.VMEM((rows, chans), bf16),
            pltpu.VMEM((rows, chans), bf16),
            pltpu.VMEM((rows, chans), bf16),
            pltpu.VMEM((1, rows), jnp.int32),
            pltpu.VMEM((tap_count, filters), f32),
            pltpu.VMEM((filters, MAXDOC), bf16),
            pltpu.VMEM((RIM, chans), bf16),
            pltpu.VMEM((RIM, chans), bf16),
            pltpu.VMEM((tiles, rows, LANES), bf16),
            pltpu.VMEM((REACH, tiles, rows, LANES), bf16),
            pltpu.VMEM((8, LANES), f32),
            pltpu.VMEM((REACH, 8, LANES), f32),
            pltpu.VMEM((RIM, chans), bf16),
            pltpu.VMEM((RIM, chans), bf16),
            pltpu.VMEM((filters // LANES, 8, LANES), f32),
            pltpu.VMEM((RIM + rows, LANES), f32),
            pltpu.VMEM((max(4, tiles // MSGS), RIM + rows, LANES), f32),
            pltpu.VMEM((tap_count, rows, LANES), f32),
            pltpu.VMEM((filters, MAXDOC), f32),
            pltpu.VMEM((tiles, REACH, LANES // fgroup * BASE, LANES), bf16),
            pltpu.VMEM((tiles, rows, LANES), f32),
            pltpu.VMEM((2, rows // 2, LANES), bf16),
            pltpu.VMEM((REACH, rows, LANES), bf16),
            pltpu.VMEM((rows, LANES), f32),
            pltpu.VMEM((2 * (tiles // MSGS), REACH, LANES // fgroup * PACK, LANES), f32),
            pltpu.VMEM((AHEAD * 2 * (tiles // MSGS), LANES // fgroup * PACK, LANES), bf16),
            pltpu.VMEM((VIA * (tiles // MSGS), rows, LANES), bf16),
            dma((3, GROUPS)),
            dma((6,)),
            dma((REACH,)),
            dma((REACH, MSGS)),
            dma((REACH,)),
            dma((REACH,)),
            dma((REACH,)),
            dma((REACH,)),
            dma,
            dma,
            dma((VIA,)),
            dma((VIA,)),
            dma((VIA,)),
        ],
        compiler_params=pltpu.CompilerParams(
            collective_id=0, has_side_effects=True, vmem_limit_bytes=48 * 1024 * 1024
        ),
    )(*(
        pltpu.with_memory_space_constraint(x, pltpu.HBM)
        for x in (gate_short, key_short, value_short, gate_long, doc_ids.reshape(1, rows), se_filter, long_filter)
    ))


def solution(mesh):
    placed = P(("groups", "ctx"), None)
    return jax.shard_map(
        body,
        mesh=mesh,
        in_specs=(placed, placed, placed, placed, P(("groups", "ctx")), P(), P()),
        out_specs=placed,
        check_vma=False,
    )
```

```python
import functools

import jax
import jax.numpy as jnp
from jax import lax
from jax.experimental import pallas as pl
from jax.experimental.pallas import tpu as pltpu
from jax.sharding import PartitionSpec as P

MAXDOC = 512
REACH = 4
RIM = 8
LANES = 128
PACK = 16
MSGS = 16
EARLY = 3
LAG1 = 2
LAG2 = 4
VIA = 2
GROUPS = 4
FIRST = 2
AHEAD = 2
BASE = 32
MESH = pl.DeviceIdType.MESH


def kernel(
    count, gs_hbm, k_hbm, v_hbm, gl_hbm, doc_hbm, se_hbm, h_hbm, out_ref,
    gs_ref, k_ref, v_ref, gl_ref, doc_ref, se_ref, h_ref, tail_k, tail_v,
    own, got, doc_out, got_doc, rim_out, rim_in, se_two, doc_ext, ext, agree,
    rev, taps, acc, near_mask, far_mask, out_mask, ring_all, close, via,
    in_sem, one_sem, send_sem, recv_sem, head_send, head_recv, doc_send, doc_recv, rim_send, rim_recv,
    via_send, via_recv, fwd_send,
):
    rows, chans = gs_ref.shape
    tap_count, filters = se_ref.shape
    fgroup = chans // filters
    per_tile = LANES // fgroup
    tiles = chans // LANES
    each = tiles // MSGS
    width = each * LANES
    half = rows // 2
    direct = MSGS - VIA
    body_rows = rows - RIM
    f32, bf16, i32 = jnp.float32, jnp.bfloat16, jnp.int32

    me = lax.axis_index("ctx")
    at = lax.rem(me, REACH)
    core = lax.rem(me, 2)
    upper = at // 2
    core_mate = me + 1 - 2 * core
    row_mate = me + 2 - 4 * upper
    has_prev = me >= REACH
    has_next = me + REACH < count
    core_filled = has_prev | (core == 1)
    row_filled = has_prev | (upper == 1)

    def local(src, dst, sem):
        return pltpu.make_async_copy(src, dst, sem)

    def piece(i, j):
        src, dst = ((k_hbm, k_ref), (v_hbm, v_ref), (gs_hbm, gs_ref))[i]
        cols = slice(j * chans // GROUPS, (j + 1) * chans // GROUPS)
        return local(src.at[:, cols], dst.at[:, cols], in_sem.at[i, j])

    doc_in = local(doc_hbm, doc_ref, one_sem.at[0])
    tails = [
        local(k_hbm.at[pl.ds(rows - RIM, RIM), :], tail_k, one_sem.at[1]),
        local(v_hbm.at[pl.ds(rows - RIM, RIM), :], tail_v, one_sem.at[2]),
    ]
    se_in = local(se_hbm, se_ref, one_sem.at[3])
    h_in = local(h_hbm, h_ref, one_sem.at[4])
    gl_in = local(gl_hbm, gl_ref, one_sem.at[5])

    for i in range(2):
        piece(i, 0).start()
    se_in.start()
    piece(2, 0).start()
    doc_in.start()
    tails[0].start()
    tails[1].start()

    barrier = pltpu.get_barrier_semaphore()

    def greet(target):
        pl.semaphore_signal(barrier, inc=1, device_id={"ctx": target}, device_id_type=MESH)

    peers = jnp.int32(0)
    for d in range(1, REACH + 1):
        pl.when(me >= d)(lambda d=d: greet(me - d))
        pl.when(me + d < count)(lambda d=d: greet(me + d))
        peers = peers + (me >= d).astype(i32) + (me + d < count).astype(i32)

    for j in (GROUPS - 1, *range(1, GROUPS - 1)):
        for i in range(3):
            piece(i, j).start()
    h_in.start()
    gl_in.start()

    lane = lax.broadcasted_iota(i32, (rows, LANES), 1)
    row = lax.broadcasted_iota(i32, (rows, LANES), 0)

    doc_in.wait()
    doc_row = jnp.broadcast_to(doc_ref[...].astype(f32), (rows, LANES))
    doc_col = doc_row.T
    doc_out[...] = doc_row[0:8]
    doc_ext[RIM:, :] = doc_col
    tails[0].wait()
    tails[1].wait()
    rim_out[...] = (tail_k[...].astype(f32) * tail_v[...].astype(f32)).astype(bf16)

    def remote(src, dst, ssem, rsem, target):
        return pltpu.make_async_remote_copy(
            src_ref=src, dst_ref=dst, send_sem=ssem, recv_sem=rsem,
            device_id={"ctx": target}, device_id_type=MESH,
        )

    def rim_copy(target):
        return remote(rim_out, rim_in, rim_send, rim_recv, target)

    def doc_copy(d, target):
        slot = REACH - d
        return remote(doc_out, got_doc.at[slot], doc_send.at[slot], doc_recv.at[slot], target)

    def msg_copy(slot, m, source, target):
        block = own if source is None else got.at[source]
        part = (pl.ds(m * each, each), pl.ds(RIM, body_rows))
        return remote(block.at[part], got.at[(slot, *part)], send_sem.at[slot], recv_sem.at[slot, m], target)

    def head_copy(slot, source, target):
        block = own if source is None else got.at[source]
        part = (pl.ds(0, tiles), pl.ds(0, RIM))
        return remote(block.at[part], got.at[(slot, *part)], head_send.at[slot], head_recv.at[slot], target)

    def send_own(copy):
        pl.when(has_next)(lambda: copy(0, None, me + REACH).start())
        pl.when(upper == 0)(lambda: copy(2, None, row_mate).start())
        pl.when(core == 0)(lambda: copy(1, None, core_mate).start())

    def msg(m):
        return lambda slot, source, target: msg_copy(slot, m, source, target)

    for tap in range(1, tap_count):
        agree[tap, RIM:, :] = (doc_ext[2 * RIM - tap : RIM + rows - tap, :] == doc_col[RIM:]).astype(f32)

    se_in.wait()
    for part in range(filters // LANES):
        se_two[part, 0:tap_count, :] = se_ref[:, part * LANES : (part + 1) * LANES]
        se_two[part, tap_count:, :] = jnp.zeros((8 - tap_count, LANES), f32)

    tiles_per_part = LANES // per_tile
    spread = lax.broadcasted_iota(i32, (8, LANES), 1) // fgroup

    def weights_of(ct):
        index = spread + lax.rem(ct, tiles_per_part) * per_tile
        return jnp.take_along_axis(se_two[ct // tiles_per_part], index, axis=1)

    def lanes_of(ct):
        return pl.ds(pl.multiple_of(ct * LANES, LANES), LANES)

    def product(ct, part):
        lanes = lanes_of(ct)
        return (k_ref[part, lanes].astype(f32) * v_ref[part, lanes].astype(f32)).astype(bf16).astype(f32)

    def await_pieces(j):
        for i in range(3):
            piece(i, j).wait()

    def short_body(j, _):
        for u in range(each):
            ct = j * each + u
            weights = weights_of(ct)
            kv = product(ct, slice(None))
            ext[u, RIM:, :] = kv
            total = kv[RIM:] * weights[0:1, :]
            for tap in range(1, tap_count):
                shifted = ext[u, 2 * RIM - tap : RIM + rows - tap, :]
                total = total + (shifted * agree[tap, RIM:, :]) * weights[tap : tap + 1, :]
            mixed = gs_ref[RIM:, lanes_of(ct)].astype(f32) * total
            own[ct, RIM:, :] = mixed.astype(bf16)
        return 0

    await_pieces(0)
    lax.fori_loop(0, FIRST, short_body, 0)

    pl.semaphore_wait(barrier, peers)
    def send_msg(j, _):
        send_own(msg(j))
        return 0

    def side(i):
        return pl.ds(i * each, each), pl.ds(RIM, body_rows)

    def via_copy(i, target):
        block = own.at[pl.ds((direct + i) * each, each), pl.ds(RIM, body_rows)]
        return remote(block, via.at[side(i)], via_send.at[i], via_recv.at[i], target)

    def fwd_copy(i, target):
        m = direct + i
        block = got.at[2, pl.ds(m * each, each), pl.ds(RIM, body_rows)]
        return remote(via.at[side(i)], block, fwd_send.at[i], recv_sem.at[2, m], target)

    send_msg(0, 0)
    pl.when(me + 1 < count)(lambda: rim_copy(me + 1).start())
    for d in range(1, REACH + 1):
        pl.when(me + d < count)(lambda d=d: doc_copy(d, me + d).start())

    lax.fori_loop(1, FIRST, send_msg, 0)
    await_pieces(GROUPS - 1)
    lax.fori_loop(direct, MSGS, short_body, 0)
    for i in range(VIA):
        pl.when((upper == 1) & has_next)(lambda i=i: via_copy(i, row_mate).start())
    lax.fori_loop(FIRST, EARLY, lambda j, c: send_msg(j, short_body(j, c)), 0)


    def clear(slot):
        got[slot] = jnp.zeros(got.shape[1:], bf16)

    @pl.when(jnp.logical_not(has_prev))
    def _():
        clear(0)
        pl.when(core == 0)(lambda: clear(1))
        pl.when(upper == 0)(lambda: clear(2))
        pl.when(upper == 0)(lambda: clear(3))

    h_in.wait()
    lag = lax.broadcasted_iota(i32, (LANES, LANES), 0)
    pos = lax.broadcasted_iota(i32, (LANES, LANES), 1)
    flip = jnp.where(lag == lax.rem(LANES - pos, LANES), 1.0, 0.0).astype(bf16)
    for d in range(REACH):
        cols = slice(d * LANES, (d + 1) * LANES)
        rev[:, cols] = jnp.dot(h_ref[:, cols], flip, preferred_element_type=f32)

    low = lane[:half] < half
    causal = lane[:half] <= row[:half]
    same_low = doc_col[:half] == doc_row[:half]
    same_high = doc_col[half:] == pltpu.roll(doc_row[:half], half, 1)
    late = same_high.astype(f32)
    early = causal.astype(f32) * same_low.astype(f32)
    near_mask[0] = jnp.where(low, early, late).astype(bf16)
    near_mask[1] = jnp.where(low, causal.astype(f32) * late, 0.0).astype(bf16)
    leader = jnp.broadcast_to(doc_row[0:1, 0:1], (rows, LANES))
    out_mask[...] = (doc_col == leader).astype(f32)

    below = [lane[0:PACK] <= row[0:PACK] + r * PACK for r in range(BASE // PACK)]

    def build_taps(ct, ring_rows):
        first = pl.multiple_of(ct * per_tile, per_tile)
        filt = rev[pl.ds(first, per_tile), :]
        for d in range(REACH):
            line = filt[:, d * LANES : (d + 1) * LANES]
            for i in range(PACK):
                ring_rows[d, pl.ds(i, per_tile, stride=PACK), :] = line if i == 0 else pltpu.roll(line, i, 1)
        zero = jnp.zeros((PACK, LANES), bf16)
        for g in range(per_tile):
            ring = [ring_rows[d, g * PACK : (g + 1) * PACK, :].astype(bf16) for d in range(REACH)]
            for r in range(BASE // PACK):
                turned = ring if r == 0 else [pltpu.roll(c, r * PACK, 1) for c in ring]
                at_row = g * BASE + r * PACK
                for w in range(REACH):
                    d = REACH - w
                    recent = turned[d] if d < REACH else zero
                    taps[ct, w, at_row : at_row + PACK, :] = jnp.where(below[r], recent, turned[d - 1])
        return ring_rows[0].astype(bf16)

    def build_ahead(q, _):
        for u in range(2 * each):
            ct = q * (2 * each) + u
            close[ct] = build_taps(ct, ring_all.at[u])
        return 0

    lax.fori_loop(0, AHEAD, build_ahead, 0)

    for w in range(REACH):
        pl.when(me >= REACH - w)(lambda w=w: doc_copy(REACH - w, core_mate).wait_recv())

        @pl.when(me < REACH - w)
        def _():
            got_doc[w] = jnp.full((8, LANES), -1.0, f32)

        source_col = jnp.broadcast_to(got_doc[w, 0:1, :], (rows, LANES)).T
        far_mask[w] = (source_col == leader).astype(bf16)
        if w == REACH - 1:
            doc_ext[0:RIM, :] = source_col[rows - RIM :]

    @pl.when(me == 0)
    def _():
        rim_in[...] = jnp.zeros((RIM, chans), bf16)

    @pl.when(me > 0)
    def _():
        rim_copy(core_mate).wait_recv()

    for tap in range(1, tap_count):
        agree[tap, 0:RIM, :] = (doc_ext[RIM - tap : 2 * RIM - tap, :] == doc_col[0:RIM]).astype(f32)

    for j in range(1, GROUPS - 1):
        await_pieces(j)

    def short_head(j, _):
        for u in range(4):
            ct = j * 4 + u
            weights = weights_of(ct)
            kv = product(ct, slice(0, RIM))
            ext[u, 0:RIM, :] = rim_in[:, lanes_of(ct)].astype(f32)
            ext[u, RIM : 2 * RIM, :] = kv
            total = kv * weights[0:1, :]
            for tap in range(1, tap_count):
                shifted = ext[u, RIM - tap : 2 * RIM - tap, :]
                total = total + (shifted * agree[tap, 0:RIM, :]) * weights[tap : tap + 1, :]
            mixed = gs_ref[0:RIM, lanes_of(ct)].astype(f32) * total
            own[ct, 0:RIM, :] = mixed.astype(bf16)
        return 0

    lax.fori_loop(0, tiles // 4, short_head, 0)
    send_own(head_copy)

    @pl.when((upper == 0) & has_next)
    def _():
        for i in range(VIA):
            via_copy(i, row_mate).wait_recv()
            fwd_copy(i, me + REACH).start()

    gl_in.wait()

    tile_group = lax.broadcasted_iota(i32, (1, LANES), 1) // fgroup
    half_group = lax.rem(tile_group, per_tile // 2)
    low_half = lax.broadcasted_iota(i32, (1, LANES), 1) < half

    def pick(result, group, groups, height, lanes):
        picked = result[0:height, lanes]
        for g in range(1, groups):
            picked = jnp.where(group == g, result[g * height : (g + 1) * height, lanes], picked)
        return picked

    def near_part(ct, close_rows):
        near = []
        for g in range(per_tile):
            ring = close_rows[g * PACK : (g + 1) * PACK]
            for r in range(half // PACK):
                turned = ring if r == 0 else pltpu.roll(ring, r * PACK, 1)
                at_mask = slice(r * PACK, (r + 1) * PACK)
                near.append(jnp.concatenate([turned * near_mask[0, at_mask], turned * near_mask[1, at_mask]], 1))
        block = own[ct]
        first_half, second_half = block[:half], block[half:]
        none = jnp.zeros((half, LANES), bf16)
        right = jnp.concatenate(
            [
                jnp.concatenate([first_half, none, none, none], 0),
                jnp.concatenate([none, first_half, second_half, none], 0),
            ],
            1,
        )
        result = jnp.dot(jnp.concatenate(near, 0), right, preferred_element_type=f32)
        acc[ct, 0:half, :] = pick(result, tile_group, per_tile, half, slice(0, LANES))
        acc[ct, half:, :] = pick(result, tile_group, per_tile, half, slice(LANES, 2 * LANES))

    slots = []
    for w in range(REACH):
        q = lax.rem(at + w, REACH)
        slots.append(lax.rem(q // 2 + upper, 2) * 2 + lax.rem(q + at, 2))

    def far(ct):
        left = jnp.concatenate([got[slots[w], ct] * far_mask[w] for w in range(REACH)], 0)
        gap = jnp.zeros((BASE, LANES), bf16)
        later = jnp.concatenate([left[BASE:], gap], 0)
        outs = []
        for h in range(2):
            if h == 0:
                pair = jnp.where(low_half, left, pltpu.roll(later, half, 1))
            else:
                pair = jnp.where(low_half, pltpu.roll(left, half, 1), later)
            wide = jnp.concatenate([pair, jnp.concatenate([pair[2 * BASE :], gap, gap], 0)], 1)
            height = per_tile // 2 * BASE
            lhs = jnp.concatenate([taps[ct, w, h * height : (h + 1) * height, :] for w in range(REACH)], 1)
            result = jnp.dot(lhs, wide, preferred_element_type=f32)
            outs.append(
                [pick(result, half_group, per_tile // 2, BASE, slice(p * LANES, (p + 1) * LANES)) for p in range(2)]
            )
        both = []
        for p in range(2):
            both.append(jnp.where(low_half, outs[0][p], pltpu.roll(outs[1][p], half, 1)))
            both.append(jnp.where(low_half, pltpu.roll(outs[0][p], half, 1), outs[1][p]))
        total = acc[ct] + jnp.concatenate(both, 0) * out_mask[...]
        out_ref[:, lanes_of(ct)] = (gl_ref[:, lanes_of(ct)].astype(f32) * total).astype(bf16)

    def step(s, _):
        @pl.when(s < MSGS - EARLY)
        def _():
            @pl.when(s < direct - EARLY)
            def _():
                short_body(s + EARLY, 0)

            send_own(msg(s + EARLY))

        def prepared(s):
            return jnp.minimum(jnp.minimum(s, (s + EARLY) // 2), MSGS // 2)

        group = prepared(s)
        fresh = prepared(s + 1) > group

        @pl.when(fresh & (group < AHEAD))
        def _():
            for u in range(2 * each):
                ct = group * (2 * each) + u
                near_part(ct, close[ct])

        @pl.when(fresh & (group >= AHEAD))
        def _():
            for u in range(2 * each):
                ct = group * (2 * each) + u
                near_part(ct, build_taps(ct, ring_all.at[u]))

        @pl.when(s < MSGS)
        def _():
            def relay(copy, row_too=True):
                pl.when(has_prev)(lambda: copy(0, None, core_mate).wait_recv())
                pl.when(has_prev & (upper == 1) & row_too)(lambda: copy(2, 0, row_mate).start())
                pl.when(has_prev & (core == 1))(lambda: copy(1, 0, core_mate).start())

            pl.when(s == EARLY)(lambda: relay(head_copy))
            relay(msg(s), s < direct)

        @pl.when((s >= LAG1) & (s < MSGS + LAG1))
        def _():
            def relay(copy):
                pl.when(row_filled)(lambda: copy(2, None, core_mate).wait_recv())
                pl.when(row_filled)(lambda: copy(3, 2, core_mate).start())

            pl.when(s == EARLY + LAG1)(lambda: relay(head_copy))
            relay(msg(s - LAG1))

        def finished(s):
            paired = (s - LAG2) // 2 * 2
            done = jnp.where(s <= MSGS, paired, s - LAG2)
            return jnp.where(s <= EARLY + LAG1 + 1, 0, done)

        def far_msgs(m, many):
            def arrive(copy):
                pl.when(core_filled)(lambda: copy(1, None, core_mate).wait_recv())
                pl.when(row_filled)(lambda: copy(3, None, core_mate).wait_recv())

            pl.when(m == 0)(lambda: arrive(head_copy))
            for i in range(many):
                arrive(msg(m + i))
            for u in range(many * each):
                far(m * each + u)

        for many in (1, 2):
            pl.when(finished(s + 1) - finished(s) == many)(lambda many=many: far_msgs(finished(s), many))

        return 0

    lax.fori_loop(0, MSGS + LAG2, step, 0)

    def drain(slot, msgs):
        part = (pl.ds(0, msgs * each), pl.ds(RIM, body_rows))
        block = own.at[part]
        remote(block, got.at[(slot, *part)], send_sem.at[slot], recv_sem.at[slot, 0], core_mate).wait_send()
        head_copy(slot, None, core_mate).wait_send()

    pl.when(has_next)(lambda: drain(0, MSGS))
    pl.when(has_prev | (core == 0))(lambda: drain(1, MSGS))
    pl.when(upper == 0)(lambda: drain(2, MSGS))
    pl.when(has_prev & (upper == 1))(lambda: drain(2, direct))
    pl.when(row_filled)(lambda: drain(3, MSGS))
    for i in range(VIA):
        pl.when((upper == 1) & has_next)(lambda i=i: via_copy(i, core_mate).wait_send())
        pl.when((upper == 0) & has_next)(lambda i=i: fwd_copy(i, core_mate).wait_send())
    pl.when(me + 1 < count)(lambda: rim_copy(core_mate).wait_send())
    for d in range(1, REACH + 1):
        pl.when(me + d < count)(lambda d=d: doc_copy(d, core_mate).wait_send())


def body(gate_short, key_short, value_short, gate_long, doc_ids, se_filter, long_filter):
    rows, chans = gate_short.shape
    tap_count, filters = se_filter.shape
    fgroup = chans // filters
    count = lax.axis_size("ctx")
    tiles = chans // LANES
    assert rows * REACH == MAXDOC and rows == LANES and count % REACH == 0
    assert tap_count <= RIM and LANES % fgroup == 0 and filters % LANES == 0
    assert tiles % MSGS == 0 and tiles % 4 == 0 and long_filter.shape[1] == MAXDOC
    bf16, f32 = jnp.bfloat16, jnp.float32
    anywhere = pl.BlockSpec(memory_space=pl.ANY)
    dma = pltpu.SemaphoreType.DMA
    return pl.pallas_call(
        functools.partial(kernel, count),
        out_shape=pltpu.VMEM((rows, chans), bf16),
        in_specs=[anywhere] * 7,
        out_specs=pl.BlockSpec(memory_space=pltpu.VMEM),
        scratch_shapes=[
            pltpu.VMEM((rows, chans), bf16),
            pltpu.VMEM((rows, chans), bf16),
            pltpu.VMEM((rows, chans), bf16),
            pltpu.VMEM((rows, chans), bf16),
            pltpu.VMEM((1, rows), jnp.int32),
            pltpu.VMEM((tap_count, filters), f32),
            pltpu.VMEM((filters, MAXDOC), bf16),
            pltpu.VMEM((RIM, chans), bf16),
            pltpu.VMEM((RIM, chans), bf16),
            pltpu.VMEM((tiles, rows, LANES), bf16),
            pltpu.VMEM((REACH, tiles, rows, LANES), bf16),
            pltpu.VMEM((8, LANES), f32),
            pltpu.VMEM((REACH, 8, LANES), f32),
            pltpu.VMEM((RIM, chans), bf16),
            pltpu.VMEM((RIM, chans), bf16),
            pltpu.VMEM((filters // LANES, 8, LANES), f32),
            pltpu.VMEM((RIM + rows, LANES), f32),
            pltpu.VMEM((max(4, tiles // MSGS), RIM + rows, LANES), f32),
            pltpu.VMEM((tap_count, rows, LANES), f32),
            pltpu.VMEM((filters, MAXDOC), f32),
            pltpu.VMEM((tiles, REACH, LANES // fgroup * BASE, LANES), bf16),
            pltpu.VMEM((tiles, rows, LANES), f32),
            pltpu.VMEM((2, rows // 2, LANES), bf16),
            pltpu.VMEM((REACH, rows, LANES), bf16),
            pltpu.VMEM((rows, LANES), f32),
            pltpu.VMEM((2 * (tiles // MSGS), REACH, LANES // fgroup * PACK, LANES), f32),
            pltpu.VMEM((AHEAD * 2 * (tiles // MSGS), LANES // fgroup * PACK, LANES), bf16),
            pltpu.VMEM((VIA * (tiles // MSGS), rows, LANES), bf16),
            dma((3, GROUPS)),
            dma((6,)),
            dma((REACH,)),
            dma((REACH, MSGS)),
            dma((REACH,)),
            dma((REACH,)),
            dma((REACH,)),
            dma((REACH,)),
            dma,
            dma,
            dma((VIA,)),
            dma((VIA,)),
            dma((VIA,)),
        ],
        compiler_params=pltpu.CompilerParams(
            collective_id=0, has_side_effects=True, vmem_limit_bytes=48 * 1024 * 1024
        ),
    )(*(
        pltpu.with_memory_space_constraint(x, pltpu.HBM)
        for x in (gate_short, key_short, value_short, gate_long, doc_ids.reshape(1, rows), se_filter, long_filter)
    ))


def solution(mesh):
    placed = P(("groups", "ctx"), None)
    return jax.shard_map(
        body,
        mesh=mesh,
        in_specs=(placed, placed, placed, placed, P(("groups", "ctx")), P(), P()),
        out_specs=placed,
        check_vma=False,
    )
```
